768 devices in a mesh: dp: 24 (over x, z_lo), space: 32 (over z_hi, y, core).
Axes of the slice: x: 4, y: 8, z: 12 (z_hi: 2, z_lo: 6; z = z_hi * 6 + z_lo), core: 2. Of those that a mesh axis runs over, the one named last changes fastest.
Arguments:
- image: bfloat16 [24, 256, 10240], P('dp', 'space'), may hold values from -6 to 6
- cotangent: bfloat16 [24, 128, 5120], P('dp', 'space'), may hold values from -6 to 6
- weight: float32 [1440, 160], P('dp'), may hold values from -0.15625 to 0.15625
- moment_one: float32 [1440, 160], P('dp'), may hold values from -0.046875 to 0.046875
- moment_two: float32 [1440, 160], P('dp'), may hold values from 2.5431316e-06 to 4.0690105e-05
Outputs:
- output: bfloat16 [24, 128, 5120], P('dp', 'space')
- grad_image: bfloat16 [24, 256, 10240], P('dp', 'space')
- new_weight: float32 [1440, 160], P('dp')
- new_moment_one: float32 [1440, 160], P('dp')
- new_moment_two: float32 [1440, 160], P('dp')
The draws below stay inside these ranges and needn't reach their ends.
All inputs are finite; a program needn't handle non-finite values.
Results may differ from the reference program's by a relative error of at most 0.0049.
Values may be sent and summed in bfloat16 or wider, within the bound.
No kernel may reach another device: no remote copies, remote signals or barrier semaphores. Data moves between devices by JAX's collectives and lax.ppermute only.
A program may use at most 32 MiB of HBM per device.

```python
import math
import jax
import jax.numpy as jnp
from jax import lax

C = 160
W = 64
BATCH = 24
H = 256
OH = 128
OW = 32
KROWS = 1440
COUNT = 98304


def block_levels(rng, shape, pieces, low, top_value):
    loudness = 1.0
    for position, blocks in pieces:
        heights = jax.random.uniform(jax.random.fold_in(jax.random.fold_in(rng, 6), position), (blocks,), jnp.float32, low / len(pieces), top_value / len(pieces))
        loudness = loudness * jnp.repeat(jnp.exp(heights), shape[position] // blocks).reshape((-1,) + (1,) * (len(shape) - 1 - position))
    return loudness


def centred(stream_key, dims, deviation, limit, pieces=(), kind=jnp.bfloat16):
    values = deviation * jax.random.normal(stream_key, dims, jnp.float32)
    if pieces:
        values = values * block_levels(stream_key, dims, pieces, -0.22, 0.18)
    return jnp.clip(values, -limit, limit).astype(kind)


def setup_inputs(seed: int = 0) -> dict:
    key_of = jax.random.split(jax.random.key(seed), 6)
    image = centred(key_of[0], (BATCH, H, W * C), 1.0, 6.0, ((0, 24), (1, 32)))
    cotangent = centred(key_of[1], (BATCH, OH, OW * C), 1.0, 6.0, ((0, 24), (1, 32)))
    weight = centred(key_of[2], (KROWS, C), KROWS ** -0.5, 0.15625, ((0, 24),), jnp.float32)
    moment_one = centred(key_of[3], (KROWS, C), (COUNT ** -0.5), 0.046875, ((0, 24),), jnp.float32)
    moment_two = jnp.clip(jnp.exp(math.log(4.069010537932627e-05) - 2.7725887 * jax.random.uniform(key_of[4], (KROWS, C), jnp.float32) ** block_levels(key_of[4], (KROWS, C), ((0, 24),), -0.2, 0.2)), 2.543131586207892e-06, 4.069010537932627e-05)
    return dict(image=image, cotangent=cotangent, weight=weight, moment_one=moment_one, moment_two=moment_two)


def convolve(sample, kernel):
    return lax.conv_general_dilated(sample[None], kernel, (2, 2), ((1, 1), (1, 1)), dimension_numbers=('NHWC', 'HWIO', 'NHWC'), precision=lax.Precision.HIGHEST)[0]

def reference(image, cotangent, weight, moment_one, moment_two):
    kernel = weight.astype(jnp.bfloat16).astype(jnp.float32).reshape(3, 3, C, C)
    image_four = image.reshape(BATCH, H, W, C)
    cotan_four = cotangent.reshape(BATCH, OH, OW, C)

    def per_sample(carried, inputs):
        sample_in, sample_cot = inputs
        forward, pullback = jax.vjp(convolve, sample_in.astype(jnp.float32), kernel)
        grad_in, grad_kernel = pullback(sample_cot.astype(jnp.float32))
        return (carried + grad_kernel, (forward.astype(jnp.bfloat16), grad_in.astype(jnp.bfloat16)))
    summed, (output, grad_image) = lax.scan(per_sample, jnp.zeros((3, 3, C, C), jnp.float32), (image_four, cotan_four))
    gradient = summed.reshape(KROWS, C) / COUNT
    new_moment_one = 0.9 * moment_one + 0.1 * gradient
    new_moment_two = 0.999 * moment_two + 0.001 * gradient * gradient
    first_hat = new_moment_one / (1.0 - 0.9 ** 10)
    second_hat = new_moment_two / (1.0 - 0.999 ** 10)
    new_weight = weight - 0.01 * (first_hat / (jnp.sqrt(second_hat) + 1e-08) + 0.01 * weight)
    output = output.reshape(BATCH, OH, OW * C)
    grad_image = grad_image.reshape(BATCH, H, W * C)
    return (output, grad_image, new_weight, new_moment_one, new_moment_two)
```

```python
import jax
import jax.numpy as jnp
from jax import lax
from jax.experimental import pallas as pl
from jax.experimental.pallas import tpu as pltpu
from jax.sharding import Mesh
from jax.sharding import PartitionSpec as P

beta_one = 0.9
beta_two = 0.999
learn_rate = 0.01
decay_rate = 0.01
epsilon = 1e-08
adam_step = 10

C = 160
COUNT = 98304
F32 = jnp.float32
BF16 = jnp.bfloat16
VM = pl.BlockSpec(memory_space=pltpu.VMEM)
SM = pl.BlockSpec(memory_space=pltpu.SMEM)

PIECE = 40
GRAD_ROWS = 6 * PIECE
SEND_ONE = GRAD_ROWS + 32
SEND_TWO = PIECE + 80


def call(kernel, outs, scratch=(), flops=0, moved=0):
    return pl.pallas_call(
        kernel,
        out_shape=outs,
        scratch_shapes=list(scratch),
        cost_estimate=pl.CostEstimate(flops=flops, bytes_accessed=moved, transcendentals=0),
    )


def tile_rows(piece, wide, groups):
    tiles = []
    for g in range(groups):
        block = piece(wide, g)
        tiles += [block[:, 160 * k : 160 * k + 160] for k in range(4)]
    return tiles


def read_block(ref, g):
    return ref[:, 640 * g : 640 * g + 640].astype(F32)


def pack(rows):
    tail = rows[:, 128:160]
    side = jnp.concatenate([tail[8 * b : 8 * b + 8] for b in range(4)], axis=1)
    return jnp.concatenate([rows[:, 0:128], side], axis=0)


def unpack(piece):
    side = piece[32:40]
    tail = jnp.concatenate([side[:, 32 * b : 32 * b + 32] for b in range(4)], axis=0)
    return jnp.concatenate([piece[0:32], tail], axis=1)


def grad_kernel(
    where_ref, image_ref, cotan_ref, below_ref, weight_ref,
    send_ref, even_ref, odd_ref, taps_ref,
    five_ref, spread_ref, sums_ref, rows_ref,
):
    tiles = tile_rows(read_block, image_ref, 16)
    even = jnp.concatenate(tiles[0::2], axis=0).astype(BF16)
    odd = jnp.concatenate(tiles[1::2], axis=0).astype(BF16)
    even_ref[...] = even
    odd_ref[...] = odd
    five_ref[...] = jnp.zeros_like(five_ref)
    five_ref[0:4] = cotan_ref[...].astype(F32)
    five_ref[4:5] = below_ref[...].astype(F32)
    out_row = lax.broadcasted_iota(jnp.int32, (24, 8), 0)
    in_row = lax.broadcasted_iota(jnp.int32, (24, 8), 1)
    pick = (2 * in_row + out_row // 8 - 1 == out_row % 8).astype(F32).astype(BF16)
    spread_ref[...] = jnp.dot(pick, five_ref[...].astype(BF16), preferred_element_type=F32)
    taps = []
    for r in range(3):
        cols = tile_rows(lambda ref, g: ref[8 * r : 8 * r + 8, 640 * g : 640 * g + 640], spread_ref, 8)
        block = jnp.concatenate(cols, axis=0).astype(BF16)
        taps_ref[r] = block
        taps.append(block)
    zeros = jnp.zeros((8, C), BF16)

    def put(r, s, left, right):
        row = (3 * r + s) * C
        sums_ref[row : row + C] = lax.dot_general(
            left, right, (((0,), (0,)), ((), ())), preferred_element_type=F32
        )

    for r in range(3):
        put(r, 1, even, taps[r])
        put(r, 2, odd, taps[r])
        put(r, 0, odd[0:248], taps[r][8:256])
    sums_ref[1440:1448] = zeros.astype(F32)
    for x in range(4):
        for core in range(2):
            for low in range(6):
                start = 30 * (2 * (6 * x + low) + core)
                piece = pack(sums_ref[start : start + 32])
                send_ref[2 * x + core, PIECE * low : PIECE * low + PIECE] = piece.astype(BF16)
    rows_ref[0:60] = weight_ref[...]
    rows_ref[60:64] = jnp.zeros((4, C), F32)
    quarter = where_ref[0]
    mine = rows_ref[0:16]
    for q in range(1, 4):
        mine = jnp.where(quarter == q, rows_ref[15 * q : 15 * q + 16], mine)
    tail = mine[:, 128:160]
    lane = lax.broadcasted_iota(jnp.int32, (16, 128), 1) // 32
    tail = jnp.where(lane == where_ref[1], jnp.concatenate([tail] * 4, axis=1), 0.0)
    both = jnp.concatenate([mine[:, 0:128], tail], axis=0).astype(BF16)
    for n in range(8):
        send_ref[n, GRAD_ROWS:SEND_ONE] = both


def first_sum_kernel(where_ref, got_ref, send_ref):
    total = got_ref[0, 0:GRAD_ROWS].astype(F32)
    for n in range(1, 8):
        total = total + got_ref[n, 0:GRAD_ROWS].astype(F32)
    total = total.astype(BF16)
    core = where_ref[2]
    heads = [got_ref[2 * x + core, GRAD_ROWS : GRAD_ROWS + 16] for x in range(4)]
    tail = got_ref[core, GRAD_ROWS + 16 : SEND_ONE].astype(F32)
    for x in range(1, 4):
        tail = tail + got_ref[2 * x + core, GRAD_ROWS + 16 : SEND_ONE].astype(F32)
    tail = tail.astype(BF16)
    for low in range(6):
        for high in range(2):
            n = 2 * low + high
            send_ref[n, 0:PIECE] = total[PIECE * low : PIECE * low + PIECE]
            for x in range(4):
                send_ref[n, PIECE + 16 * x : PIECE + 16 * x + 16] = heads[x]
            send_ref[n, PIECE + 64 : SEND_TWO] = tail


def second_sum_kernel(got_ref, send_ref):
    total = got_ref[0, 0:PIECE].astype(F32)
    for n in range(1, 12):
        total = total + got_ref[n, 0:PIECE].astype(F32)
    total = total.astype(BF16)
    for n in range(16):
        send_ref[n] = total


def conv_kernel(
    where_ref, image_ref, above_ref, even_ref, odd_ref, taps_ref, own_ref, other_ref,
    out_ref, grad_ref,
    kernel_ref, shift_ref, roll_ref,
):
    core = where_ref[2]
    for x in range(4):
        for low in range(6):
            for c in range(2):
                for high in range(2):
                    n = 2 * low + high
                    own = own_ref[n, PIECE:SEND_TWO].astype(F32)
                    other = other_ref[n, PIECE:SEND_TWO].astype(F32)
                    block = jnp.where(core == c, own, other)
                    start = 60 * (6 * x + low) + 15 * (2 * c + high)
                    kernel_ref[start : start + 16] = jnp.concatenate(
                        [block[16 * x : 16 * x + 16], block[64:80, 32 * x : 32 * x + 32]], axis=1
                    )

    def tap(r, s):
        row = (3 * r + s) * C
        return kernel_ref[row : row + C].astype(BF16)

    def dot(left, right):
        return jnp.dot(left, right, preferred_element_type=F32)

    def dot_t(left, right):
        return lax.dot_general(left, right, (((1,), (1,)), ((), ())), preferred_element_type=F32)

    zeros = jnp.zeros((8, C), BF16)
    even = even_ref[...]
    odd = odd_ref[...]
    odd_before = jnp.concatenate([zeros, odd[0:248]], axis=0)
    shift_ref[0:1] = above_ref[...].astype(F32)
    shift_ref[1:9] = image_ref[...].astype(F32)
    tiles = tile_rows(lambda ref, g: ref[0:8, 640 * g : 640 * g + 640], shift_ref, 16)
    even_down = jnp.concatenate(tiles[0::2], axis=0).astype(BF16)
    odd_down = jnp.concatenate(tiles[1::2], axis=0).astype(BF16)
    odd_down_before = jnp.concatenate([zeros, odd_down[0:248]], axis=0)
    roll_ref[0:256] = dot(even, tap(2, 1)) + dot(odd, tap(2, 2)) + dot(odd_before, tap(2, 0))
    roll_ref[256:264] = jnp.zeros((8, C), F32)
    total = dot(even_down, tap(0, 1)) + dot(odd_down, tap(0, 2)) + dot(odd_down_before, tap(0, 0))
    total = total + dot(even, tap(1, 1)) + dot(odd, tap(1, 2)) + dot(odd_before, tap(1, 0))
    total = total + roll_ref[1:257]
    for g in range(8):
        wide = jnp.concatenate(
            [total[32 * g + 8 * k : 32 * g + 8 * k + 8] for k in range(4)], axis=1
        )
        rows = jnp.concatenate([wide[2 * i : 2 * i + 1] for i in range(4)], axis=0)
        out_ref[:, 640 * g : 640 * g + 640] = rows.astype(BF16)
    taps = [taps_ref[r] for r in range(3)]
    after = [jnp.concatenate([t[8:256], zeros], axis=0) for t in taps]
    grad_even = dot_t(taps[0], tap(0, 1)) + dot_t(taps[1], tap(1, 1)) + dot_t(taps[2], tap(2, 1))
    grad_odd = dot_t(taps[0], tap(0, 2)) + dot_t(taps[1], tap(1, 2)) + dot_t(taps[2], tap(2, 2))
    for r in range(3):
        grad_odd = grad_odd + dot_t(after[r], tap(r, 0))
    for g in range(16):
        parts = []
        for k in range(2):
            row = 16 * g + 8 * k
            parts += [grad_even[row : row + 8], grad_odd[row : row + 8]]
        grad_ref[:, 640 * g : 640 * g + 640] = jnp.concatenate(parts, axis=1).astype(BF16)


def adam_kernel(got_ref, weight_ref, one_ref, two_ref, new_weight_ref, new_one_ref, new_two_ref, sums_ref):
    for core in range(2):
        total = got_ref[core].astype(F32)
        for y in range(1, 8):
            total = total + got_ref[2 * y + core].astype(F32)
        sums_ref[30 * core : 30 * core + 32] = unpack(total)
    gradient = sums_ref[0:60] / float(COUNT)
    weight = weight_ref[...]
    new_one = beta_one * one_ref[...] + (1.0 - beta_one) * gradient
    new_two = beta_two * two_ref[...] + (1.0 - beta_two) * gradient * gradient
    first_hat = new_one / (1.0 - beta_one**adam_step)
    second_hat = new_two / (1.0 - beta_two**adam_step)
    new_weight_ref[...] = weight - learn_rate * (
        first_hat / (jnp.sqrt(second_hat) + epsilon) + decay_rate * weight
    )
    new_one_ref[...] = new_one
    new_two_ref[...] = new_two


def from_behind(block, distance):
    axes = ("zhi", "y", "core")
    route = [(i - distance, i) for i in range(32) if 0 <= i - distance < 32]
    return lax.ppermute(block, axes, route)


def body(image, cotangent, weight, moment_one, moment_two):
    shape = jax.ShapeDtypeStruct
    image = image.reshape(8, 64 * C)
    cotangent = cotangent.reshape(4, 32 * C)
    below = from_behind(cotangent[0:1], -1)
    above = from_behind(image[7:8], 1)
    core = lax.axis_index("core")
    place = jnp.stack([2 * core + lax.axis_index("zhi"), lax.axis_index("x"), core]).astype(jnp.int32)
    send_one, even, odd, taps = pl.pallas_call(
        grad_kernel,
        in_specs=[SM, VM, VM, VM, VM],
        out_specs=[VM] * 4,
        out_shape=[
            shape((8, SEND_ONE, 128), BF16),
            shape((256, C), BF16),
            shape((256, C), BF16),
            shape((3, 256, C), BF16),
        ],
        scratch_shapes=[
            pltpu.VMEM((8, 32 * C), F32),
            pltpu.VMEM((24, 32 * C), F32),
            pltpu.VMEM((1448, C), F32),
            pltpu.VMEM((64, C), F32),
        ],
        name="kernel_grad",
    )(place, image, cotangent, below, weight)
    got_one = lax.all_to_all(send_one, ("x", "core"), 0, 0, tiled=True)
    send_two = pl.pallas_call(
        first_sum_kernel,
        in_specs=[SM, VM],
        out_specs=VM,
        out_shape=shape((12, SEND_TWO, 128), BF16),
        name="first_sum",
    )(place, got_one)
    got_two = lax.all_to_all(send_two, ("zlo", "zhi"), 0, 0, tiled=True)
    other = lax.ppermute(got_two, "core", [(0, 1), (1, 0)])
    send_three = pl.pallas_call(
        second_sum_kernel,
        in_specs=[VM],
        out_specs=VM,
        out_shape=shape((16, PIECE, 128), BF16),
        name="second_sum",
    )(got_two)
    got_three = lax.all_to_all(send_three, ("y", "core"), 0, 0, tiled=True)
    output, grad_image = pl.pallas_call(
        conv_kernel,
        in_specs=[SM] + [VM] * 7,
        out_specs=[VM] * 2,
        out_shape=[shape((4, 32 * C), BF16), shape((8, 64 * C), BF16)],
        scratch_shapes=[
            pltpu.VMEM((1448, C), F32),
            pltpu.VMEM((16, 64 * C), F32),
            pltpu.VMEM((264, C), F32),
        ],
        name="conv_both",
    )(place, image, above, even, odd, taps, got_two, other)
    new_weight, new_one, new_two = pl.pallas_call(
        adam_kernel,
        in_specs=[VM] * 4,
        out_specs=[VM] * 3,
        out_shape=[shape((60, C), F32)] * 3,
        scratch_shapes=[pltpu.VMEM((64, C), F32)],
        name="adam",
    )(got_three, weight, moment_one, moment_two)
    return (output[None], grad_image[None], new_weight, new_one, new_two)


def solution(mesh):
    fine = Mesh(mesh.devices.reshape(4, 6, 2, 8, 2), ("x", "zlo", "zhi", "y", "core"))
    dp, space = ("x", "zlo"), ("zhi", "y", "core")
    specs = (P(dp, space, None), P(dp, space, None), P(dp, None), P(dp, None), P(dp, None))
    return jax.shard_map(body, mesh=fine, in_specs=specs, out_specs=specs, check_vma=False)
```

```python
import jax
import jax.numpy as jnp
from jax import lax
from jax.experimental import pallas as pl
from jax.experimental.pallas import tpu as pltpu
from jax.sharding import Mesh
from jax.sharding import PartitionSpec as P


beta_one = 0.9
beta_two = 0.999
learn_rate = 0.01
decay_rate = 0.01
epsilon = 1e-08
adam_step = 10

C = 160
COUNT = 98304
F32 = jnp.float32
BF16 = jnp.bfloat16
VM = pl.BlockSpec(memory_space=pltpu.VMEM)

PIECE = 40
GRAD_ROWS = 6 * PIECE
SEND_ONE = GRAD_ROWS + 32
SEND_TWO = PIECE + 80


def call(kernel, outs, scratch=(), limit=16):
    one = not isinstance(outs, list)
    return pl.pallas_call(
        kernel,
        out_shape=outs,
        out_specs=VM if one else [VM] * len(outs),
        scratch_shapes=list(scratch),
        compiler_params=pltpu.CompilerParams(vmem_limit_bytes=limit << 20),
    )


def tile_rows(piece, wide, groups):
    tiles = []
    for g in range(groups):
        block = piece(wide, g)
        tiles += [block[:, 160 * k : 160 * k + 160] for k in range(4)]
    return tiles


def read_block(ref, g):
    return ref[:, 640 * g : 640 * g + 640].astype(F32)


def pack(rows):
    tail = rows[:, 128:160]
    side = jnp.concatenate([tail[8 * b : 8 * b + 8] for b in range(4)], axis=1)
    return jnp.concatenate([rows[:, 0:128], side], axis=0)


def unpack(piece):
    side = piece[32:40]
    tail = jnp.concatenate([side[:, 32 * b : 32 * b + 32] for b in range(4)], axis=0)
    return jnp.concatenate([piece[0:32], tail], axis=1)


def grad_kernel(
    image_ref, cotan_ref, below_ref, weight_ref,
    send_ref, even_ref, odd_ref, taps_ref,
    five_ref, spread_ref, sums_ref, rows_ref,
):
    tiles = tile_rows(read_block, image_ref, 16)
    even = jnp.concatenate(tiles[0::2], axis=0).astype(BF16)
    odd = jnp.concatenate(tiles[1::2], axis=0).astype(BF16)
    even_ref[...] = even
    odd_ref[...] = odd
    five_ref[...] = jnp.zeros_like(five_ref)
    five_ref[0:4] = cotan_ref[...].astype(F32)
    five_ref[4:5] = below_ref[...].astype(F32)
    out_row = lax.broadcasted_iota(jnp.int32, (24, 8), 0)
    in_row = lax.broadcasted_iota(jnp.int32, (24, 8), 1)
    pick = (2 * in_row + out_row // 8 - 1 == out_row % 8).astype(F32).astype(BF16)
    spread_ref[...] = jnp.dot(pick, five_ref[...].astype(BF16), preferred_element_type=F32)
    taps = []
    for r in range(3):
        cols = tile_rows(lambda ref, g: ref[8 * r : 8 * r + 8, 640 * g : 640 * g + 640], spread_ref, 8)
        block = jnp.concatenate(cols, axis=0).astype(BF16)
        taps_ref[r] = block
        taps.append(block)
    zeros = jnp.zeros((8, C), BF16)

    def put(r, s, left, right):
        row = (3 * r + s) * C
        sums_ref[row : row + C] = lax.dot_general(
            left, right, (((0,), (0,)), ((), ())), preferred_element_type=F32
        )

    for r in range(3):
        put(r, 1, even, taps[r])
        put(r, 2, odd, taps[r])
        put(r, 0, odd[0:248], taps[r][8:256])
    sums_ref[1440:1448] = zeros.astype(F32)
    for x in range(4):
        for core in range(2):
            for low in range(6):
                start = 30 * (2 * (6 * x + low) + core)
                piece = pack(sums_ref[start : start + 32])
                send_ref[2 * x + core, PIECE * low : PIECE * low + PIECE] = piece.astype(BF16)
    rows_ref[0:60] = weight_ref[...]
    rows_ref[60:64] = jnp.zeros((4, C), F32)
    quarter = 2 * lax.axis_index("core") + lax.axis_index("zhi")
    mine = rows_ref[0:16]
    for q in range(1, 4):
        mine = jnp.where(quarter == q, rows_ref[15 * q : 15 * q + 16], mine)
    tail = mine[:, 128:160]
    lane = lax.broadcasted_iota(jnp.int32, (16, 128), 1) // 32
    tail = jnp.where(lane == lax.axis_index("x"), jnp.concatenate([tail] * 4, axis=1), 0.0)
    both = jnp.concatenate([mine[:, 0:128], tail], axis=0).astype(BF16)
    for n in range(8):
        send_ref[n, GRAD_ROWS:SEND_ONE] = both


def first_sum_kernel(got_ref, send_ref):
    total = got_ref[0, 0:GRAD_ROWS].astype(F32)
    for n in range(1, 8):
        total = total + got_ref[n, 0:GRAD_ROWS].astype(F32)
    total = total.astype(BF16)
    core = lax.axis_index("core")
    heads = [got_ref[2 * x + core, GRAD_ROWS : GRAD_ROWS + 16] for x in range(4)]
    tail = got_ref[core, GRAD_ROWS + 16 : SEND_ONE].astype(F32)
    for x in range(1, 4):
        tail = tail + got_ref[2 * x + core, GRAD_ROWS + 16 : SEND_ONE].astype(F32)
    tail = tail.astype(BF16)
    for low in range(6):
        for high in range(2):
            n = 2 * low + high
            send_ref[n, 0:PIECE] = total[PIECE * low : PIECE * low + PIECE]
            for x in range(4):
                send_ref[n, PIECE + 16 * x : PIECE + 16 * x + 16] = heads[x]
            send_ref[n, PIECE + 64 : SEND_TWO] = tail


def second_sum_kernel(got_ref, send_ref):
    total = got_ref[0, 0:PIECE].astype(F32)
    for n in range(1, 12):
        total = total + got_ref[n, 0:PIECE].astype(F32)
    total = total.astype(BF16)
    for n in range(16):
        send_ref[n] = total


def conv_kernel(
    image_ref, above_ref, even_ref, odd_ref, taps_ref, own_ref, other_ref,
    out_ref, grad_ref,
    kernel_ref, shift_ref, roll_ref,
):
    core = lax.axis_index("core")
    for x in range(4):
        for low in range(6):
            for c in range(2):
                for high in range(2):
                    n = 2 * low + high
                    own = own_ref[n, PIECE:SEND_TWO].astype(F32)
                    other = other_ref[n, PIECE:SEND_TWO].astype(F32)
                    block = jnp.where(core == c, own, other)
                    start = 60 * (6 * x + low) + 15 * (2 * c + high)
                    kernel_ref[start : start + 16] = jnp.concatenate(
                        [block[16 * x : 16 * x + 16], block[64:80, 32 * x : 32 * x + 32]], axis=1
                    )

    def tap(r, s):
        row = (3 * r + s) * C
        return kernel_ref[row : row + C].astype(BF16)

    def dot(left, right):
        return jnp.dot(left, right, preferred_element_type=F32)

    def dot_t(left, right):
        return lax.dot_general(left, right, (((1,), (1,)), ((), ())), preferred_element_type=F32)

    zeros = jnp.zeros((8, C), BF16)
    even = even_ref[...]
    odd = odd_ref[...]
    odd_before = jnp.concatenate([zeros, odd[0:248]], axis=0)
    shift_ref[0:1] = above_ref[...].astype(F32)
    shift_ref[1:9] = image_ref[...].astype(F32)
    tiles = tile_rows(lambda ref, g: ref[0:8, 640 * g : 640 * g + 640], shift_ref, 16)
    even_down = jnp.concatenate(tiles[0::2], axis=0).astype(BF16)
    odd_down = jnp.concatenate(tiles[1::2], axis=0).astype(BF16)
    odd_down_before = jnp.concatenate([zeros, odd_down[0:248]], axis=0)
    roll_ref[0:256] = dot(even, tap(2, 1)) + dot(odd, tap(2, 2)) + dot(odd_before, tap(2, 0))
    roll_ref[256:264] = jnp.zeros((8, C), F32)
    total = dot(even_down, tap(0, 1)) + dot(odd_down, tap(0, 2)) + dot(odd_down_before, tap(0, 0))
    total = total + dot(even, tap(1, 1)) + dot(odd, tap(1, 2)) + dot(odd_before, tap(1, 0))
    total = total + roll_ref[1:257]
    for g in range(8):
        wide = jnp.concatenate(
            [total[32 * g + 8 * k : 32 * g + 8 * k + 8] for k in range(4)], axis=1
        )
        rows = jnp.concatenate([wide[2 * i : 2 * i + 1] for i in range(4)], axis=0)
        out_ref[:, 640 * g : 640 * g + 640] = rows.astype(BF16)
    taps = [taps_ref[r] for r in range(3)]
    after = [jnp.concatenate([t[8:256], zeros], axis=0) for t in taps]
    grad_even = dot_t(taps[0], tap(0, 1)) + dot_t(taps[1], tap(1, 1)) + dot_t(taps[2], tap(2, 1))
    grad_odd = dot_t(taps[0], tap(0, 2)) + dot_t(taps[1], tap(1, 2)) + dot_t(taps[2], tap(2, 2))
    for r in range(3):
        grad_odd = grad_odd + dot_t(after[r], tap(r, 0))
    for g in range(16):
        parts = []
        for k in range(2):
            row = 16 * g + 8 * k
            parts += [grad_even[row : row + 8], grad_odd[row : row + 8]]
        grad_ref[:, 640 * g : 640 * g + 640] = jnp.concatenate(parts, axis=1).astype(BF16)


def adam_kernel(got_ref, weight_ref, one_ref, two_ref, new_weight_ref, new_one_ref, new_two_ref, sums_ref):
    for core in range(2):
        total = got_ref[core].astype(F32)
        for y in range(1, 8):
            total = total + got_ref[2 * y + core].astype(F32)
        sums_ref[30 * core : 30 * core + 32] = unpack(total)
    gradient = sums_ref[0:60] / float(COUNT)
    weight = weight_ref[...]
    new_one = beta_one * one_ref[...] + (1.0 - beta_one) * gradient
    new_two = beta_two * two_ref[...] + (1.0 - beta_two) * gradient * gradient
    first_hat = new_one / (1.0 - beta_one**adam_step)
    second_hat = new_two / (1.0 - beta_two**adam_step)
    new_weight_ref[...] = weight - learn_rate * (
        first_hat / (jnp.sqrt(second_hat) + epsilon) + decay_rate * weight
    )
    new_one_ref[...] = new_one
    new_two_ref[...] = new_two


def from_behind(block, distance):
    axes = ("zhi", "y", "core")
    route = [(i - distance, i) for i in range(32) if 0 <= i - distance < 32]
    return lax.ppermute(block, axes, route)


def body(image, cotangent, weight, moment_one, moment_two):
    shape = jax.ShapeDtypeStruct
    image = image.reshape(8, 64 * C)
    cotangent = cotangent.reshape(4, 32 * C)
    below = from_behind(cotangent[0:1], -1)
    above = from_behind(image[7:8], 1)
    send_one, even, odd, taps = call(
        grad_kernel,
        [
            shape((8, SEND_ONE, 128), BF16),
            shape((256, C), BF16),
            shape((256, C), BF16),
            shape((3, 256, C), BF16),
        ],
        [
            pltpu.VMEM((8, 32 * C), F32),
            pltpu.VMEM((24, 32 * C), F32),
            pltpu.VMEM((1448, C), F32),
            pltpu.VMEM((64, C), F32),
        ],
    )(image, cotangent, below, weight)
    got_one = lax.all_to_all(send_one, ("x", "core"), 0, 0, tiled=True)
    send_two = call(first_sum_kernel, shape((12, SEND_TWO, 128), BF16))(got_one)
    got_two = lax.all_to_all(send_two, ("zlo", "zhi"), 0, 0, tiled=True)
    other = lax.ppermute(got_two, "core", [(0, 1), (1, 0)])
    send_three = call(second_sum_kernel, shape((16, PIECE, 128), BF16))(got_two)
    got_three = lax.all_to_all(send_three, ("y", "core"), 0, 0, tiled=True)
    output, grad_image = call(
        conv_kernel,
        [shape((4, 32 * C), BF16), shape((8, 64 * C), BF16)],
        [
            pltpu.VMEM((1448, C), F32),
            pltpu.VMEM((16, 64 * C), F32),
            pltpu.VMEM((264, C), F32),
        ],
    )(image, above, even, odd, taps, got_two, other)
    new_weight, new_one, new_two = call(
        adam_kernel, [shape((60, C), F32)] * 3, [pltpu.VMEM((64, C), F32)]
    )(got_three, weight, moment_one, moment_two)
    return (output[None], grad_image[None], new_weight, new_one, new_two)


def solution(mesh):
    fine = Mesh(mesh.devices.reshape(4, 6, 2, 8, 2), ("x", "zlo", "zhi", "y", "core"))
    dp, space = ("x", "zlo"), ("zhi", "y", "core")
    specs = (P(dp, space, None), P(dp, space, None), P(dp, None), P(dp, None), P(dp, None))

    return jax.shard_map(body, mesh=fine, in_specs=specs, out_specs=specs, check_vma=False)
```

```python
import jax
import jax.numpy as jnp
from jax import lax
from jax.experimental import pallas as pl
from jax.experimental.pallas import tpu as pltpu
from jax.sharding import Mesh
from jax.sharding import PartitionSpec as P


beta_one = 0.9
beta_two = 0.999
learn_rate = 0.01
decay_rate = 0.01
epsilon = 1e-08
adam_step = 10

C = 160
COUNT = 98304
F32 = jnp.float32
BF16 = jnp.bfloat16
VM = pl.BlockSpec(memory_space=pltpu.VMEM)

PIECE = 40
GRAD_ROWS = 6 * PIECE


def call(kernel, outs, scratch=(), limit=16):
    one = not isinstance(outs, list)
    return pl.pallas_call(
        kernel,
        out_shape=outs,
        out_specs=VM if one else [VM] * len(outs),
        scratch_shapes=list(scratch),
        compiler_params=pltpu.CompilerParams(vmem_limit_bytes=limit << 20),
    )


def tile_rows(piece, wide, groups):
    tiles = []
    for g in range(groups):
        block = piece(wide, g)
        tiles += [block[:, 160 * k : 160 * k + 160] for k in range(4)]
    return tiles


def read_block(ref, g):
    return ref[:, 640 * g : 640 * g + 640].astype(F32)


def pack(rows):
    tail = rows[:, 128:160]
    side = jnp.concatenate([tail[8 * b : 8 * b + 8] for b in range(4)], axis=1)
    return jnp.concatenate([rows[:, 0:128], side], axis=0)


def unpack(piece):
    side = piece[32:40]
    tail = jnp.concatenate([side[:, 32 * b : 32 * b + 32] for b in range(4)], axis=0)
    return jnp.concatenate([piece[0:32], tail], axis=1)


def prepare_kernel(image_ref, weight_ref, even_ref, odd_ref, half_ref, rows_ref):
    tiles = tile_rows(read_block, image_ref, 16)
    even_ref[...] = jnp.concatenate(tiles[0::2], axis=0).astype(BF16)
    odd_ref[...] = jnp.concatenate(tiles[1::2], axis=0).astype(BF16)
    rows_ref[0:60] = weight_ref[...]
    rows_ref[60:64] = jnp.zeros((4, C), F32)
    mine = jnp.where(lax.axis_index("core") == 0, rows_ref[0:32], rows_ref[30:62])
    half_ref[0] = pack(mine).astype(BF16)


def grad_kernel(
    even_ref, odd_ref, cotan_ref, below_ref,
    send_ref, taps_ref,
    five_ref, spread_ref, sums_ref,
):
    even = even_ref[...]
    odd = odd_ref[...]
    five_ref[...] = jnp.zeros_like(five_ref)
    five_ref[0:4] = cotan_ref[...].astype(F32)
    five_ref[4:5] = below_ref[0:1].astype(F32)
    out_row = lax.broadcasted_iota(jnp.int32, (24, 8), 0)
    in_row = lax.broadcasted_iota(jnp.int32, (24, 8), 1)
    pick = (2 * in_row + out_row // 8 - 1 == out_row % 8).astype(F32).astype(BF16)
    spread_ref[...] = jnp.dot(pick, five_ref[...].astype(BF16), preferred_element_type=F32)
    taps = []
    for r in range(3):
        cols = tile_rows(lambda ref, g: ref[8 * r : 8 * r + 8, 640 * g : 640 * g + 640], spread_ref, 8)
        block = jnp.concatenate(cols, axis=0).astype(BF16)
        taps_ref[r] = block
        taps.append(block)
    zeros = jnp.zeros((8, C), BF16)

    def put(r, s, left, right):
        row = (3 * r + s) * C
        sums_ref[row : row + C] = lax.dot_general(
            left, right, (((0,), (0,)), ((), ())), preferred_element_type=F32
        )

    for r in range(3):
        put(r, 1, even, taps[r])
        put(r, 2, odd, taps[r])
        put(r, 0, odd[0:248], taps[r][8:256])
    sums_ref[1440:1448] = zeros.astype(F32)
    for x in range(4):
        for core in range(2):
            for low in range(6):
                start = 30 * (2 * (6 * x + low) + core)
                piece = pack(sums_ref[start : start + 32])
                send_ref[2 * x + core, PIECE * low : PIECE * low + PIECE] = piece.astype(BF16)


def first_sum_kernel(got_ref, send_ref):
    total = got_ref[0].astype(F32)
    for n in range(1, 8):
        total = total + got_ref[n].astype(F32)
    total = total.astype(BF16)
    for n in range(12):
        send_ref[n] = total[PIECE * (n // 2) : PIECE * (n // 2) + PIECE]


def join_kernel(*refs):
    at = 0
    for ref in refs[:-1]:
        refs[-1][at : at + ref.shape[0]] = ref[...]
        at += ref.shape[0]


def decay_kernel(weight_ref, one_ref, two_ref, kept_ref, kept_one_ref, kept_two_ref):
    kept_ref[...] = weight_ref[...] - learn_rate * decay_rate * weight_ref[...]
    kept_one_ref[...] = beta_one * one_ref[...]
    kept_two_ref[...] = beta_two * two_ref[...]


def down_kernel(image_ref, above_ref, even_ref, odd_ref, shift_ref):
    shift_ref[0:1] = above_ref[...].astype(F32)
    shift_ref[1:9] = image_ref[...].astype(F32)
    tiles = tile_rows(lambda ref, g: ref[0:8, 640 * g : 640 * g + 640], shift_ref, 16)
    even_ref[...] = jnp.concatenate(tiles[0::2], axis=0).astype(BF16)
    odd_ref[...] = jnp.concatenate(tiles[1::2], axis=0).astype(BF16)


def second_sum_kernel(got_ref, send_ref):
    total = got_ref[0].astype(F32)
    for n in range(1, 12):
        total = total + got_ref[n].astype(F32)
    total = total.astype(BF16)
    for n in range(16):
        send_ref[n] = total


def conv_kernel(
    even_ref, odd_ref, even_down_ref, odd_down_ref, taps_ref, own_ref, other_ref,
    out_ref, grad_ref,
    kernel_ref, roll_ref,
):
    mine, low_mine, core_mine = lax.axis_index("x"), lax.axis_index("zlo"), lax.axis_index("core")
    for x in range(4):
        apart = jnp.where(mine + x == 3, 2, jnp.where(mine // 2 == x // 2, 1, 3))
        apart = jnp.where(mine == x, 0, apart)
        for low in range(6):
            pair = lax.rem(low_mine // 2 + 3 - low // 2, 3)
            place = 6 * apart + 2 * pair + lax.rem(low_mine + low, 2)
            own = own_ref[place].astype(F32)
            other = other_ref[place].astype(F32)
            for core in range(2):
                start = 30 * (2 * (6 * x + low) + core)
                kernel_ref[start : start + 32] = unpack(jnp.where(core_mine == core, own, other))

    def tap(r, s):
        row = (3 * r + s) * C
        return kernel_ref[row : row + C].astype(BF16)

    def dot(left, right):
        return jnp.dot(left, right, preferred_element_type=F32)

    def dot_t(left, right):
        return lax.dot_general(left, right, (((1,), (1,)), ((), ())), preferred_element_type=F32)

    zeros = jnp.zeros((8, C), BF16)
    even = even_ref[...]
    odd = odd_ref[...]
    odd_before = jnp.concatenate([zeros, odd[0:248]], axis=0)
    even_down = even_down_ref[...]
    odd_down = odd_down_ref[...]
    odd_down_before = jnp.concatenate([zeros, odd_down[0:248]], axis=0)
    roll_ref[0:256] = dot(even, tap(2, 1)) + dot(odd, tap(2, 2)) + dot(odd_before, tap(2, 0))
    roll_ref[256:264] = jnp.zeros((8, C), F32)
    total = dot(even_down, tap(0, 1)) + dot(odd_down, tap(0, 2)) + dot(odd_down_before, tap(0, 0))
    total = total + dot(even, tap(1, 1)) + dot(odd, tap(1, 2)) + dot(odd_before, tap(1, 0))
    total = total + roll_ref[1:257]
    for g in range(8):
        wide = jnp.concatenate(
            [total[32 * g + 8 * k : 32 * g + 8 * k + 8] for k in range(4)], axis=1
        )
        rows = jnp.concatenate([wide[2 * i : 2 * i + 1] for i in range(4)], axis=0)
        out_ref[:, 640 * g : 640 * g + 640] = rows.astype(BF16)
    taps = [taps_ref[r] for r in range(3)]
    after = [jnp.concatenate([t[8:256], zeros], axis=0) for t in taps]
    grad_even = dot_t(taps[0], tap(0, 1)) + dot_t(taps[1], tap(1, 1)) + dot_t(taps[2], tap(2, 1))
    grad_odd = dot_t(taps[0], tap(0, 2)) + dot_t(taps[1], tap(1, 2)) + dot_t(taps[2], tap(2, 2))
    for r in range(3):
        grad_odd = grad_odd + dot_t(after[r], tap(r, 0))
    for g in range(16):
        parts = []
        for k in range(2):
            row = 16 * g + 8 * k
            parts += [grad_even[row : row + 8], grad_odd[row : row + 8]]
        grad_ref[:, 640 * g : 640 * g + 640] = jnp.concatenate(parts, axis=1).astype(BF16)


def adam_kernel(got_ref, weight_ref, one_ref, two_ref, new_weight_ref, new_one_ref, new_two_ref, sums_ref):
    for core in range(2):
        total = got_ref[core].astype(F32)
        for y in range(1, 8):
            total = total + got_ref[2 * y + core].astype(F32)
        sums_ref[30 * core : 30 * core + 32] = unpack(total)
    gradient = sums_ref[0:60] / float(COUNT)
    new_one = one_ref[...] + (1.0 - beta_one) * gradient
    new_two = two_ref[...] + (1.0 - beta_two) * gradient * gradient
    first_hat = new_one / (1.0 - beta_one**adam_step)
    second_hat = new_two / (1.0 - beta_two**adam_step)
    new_weight_ref[...] = weight_ref[...] - learn_rate * (
        first_hat / (jnp.sqrt(second_hat) + epsilon)
    )
    new_one_ref[...] = new_one
    new_two_ref[...] = new_two


def from_behind(block, distance):
    axes = ("zhi", "y", "core")
    route = [(i - distance, i) for i in range(32) if 0 <= i - distance < 32]
    return lax.ppermute(block, axes, route)


def body(image, cotangent, weight, moment_one, moment_two):
    shape = jax.ShapeDtypeStruct
    columns = shape((256, C), BF16)
    image = image.reshape(8, 64 * C)
    cotangent = cotangent.reshape(4, 32 * C)

    def join(*blocks):
        rows = sum(block.shape[0] for block in blocks)
        return call(join_kernel, shape((rows, PIECE, 128), BF16))(*blocks)

    def exchange(block, axis, source):
        route = [(source(i), i) for i in range(lax.axis_size(axis))]
        return lax.ppermute(block, axis, route)

    below = from_behind(cotangent, -1)
    even, odd, half = call(
        prepare_kernel, [columns, columns, shape((1, PIECE, 128), BF16)], [pltpu.VMEM((64, C), F32)]
    )(image, weight)
    send_one, taps = call(
        grad_kernel,
        [shape((8, GRAD_ROWS, 128), BF16), shape((3, 256, C), BF16)],
        [
            pltpu.VMEM((8, 32 * C), F32),
            pltpu.VMEM((24, 32 * C), F32),
            pltpu.VMEM((1448, C), F32),
        ],
    )(even, odd, cotangent, below)
    got_one = lax.all_to_all(send_one, ("x", "core"), 0, 0, tiled=True)
    two = join(half, exchange(half, "zlo", lambda i: i ^ 1))
    next_two = exchange(two, "zlo", lambda i: (i - 2) % 6)
    last_two = exchange(two, "zlo", lambda i: (i - 4) % 6)
    kept = call(decay_kernel, [shape((60, C), F32)] * 3)(weight, moment_one, moment_two)
    send_two = call(first_sum_kernel, shape((12, PIECE, 128), BF16))(got_one)
    got_two = lax.all_to_all(send_two, ("zlo", "zhi"), 0, 0, tiled=True)
    above = from_behind(image[7:8], 1)
    six = join(two, next_two, last_two)
    twelve = join(six, exchange(six, "x", lambda i: i ^ 1))
    across = exchange(twelve, "x", lambda i: 3 - i)
    downs = call(down_kernel, [columns] * 2, [pltpu.VMEM((16, 64 * C), F32)])(image, above)
    send_three = call(second_sum_kernel, shape((16, PIECE, 128), BF16))(got_two)
    got_three = lax.all_to_all(send_three, ("y", "core"), 0, 0, tiled=True)
    own = join(twelve, across)
    other = exchange(own, "core", lambda i: 1 - i)
    output, grad_image = call(
        conv_kernel,
        [shape((4, 32 * C), BF16), shape((8, 64 * C), BF16)],
        [pltpu.VMEM((1448, C), F32), pltpu.VMEM((264, C), F32)],
    )(even, odd, *downs, taps, own, other)
    new_weight, new_one, new_two = call(
        adam_kernel, [shape((60, C), F32)] * 3, [pltpu.VMEM((64, C), F32)]
    )(got_three, *kept)
    return (output[None], grad_image[None], new_weight, new_one, new_two)


def solution(mesh):
    fine = Mesh(mesh.devices.reshape(4, 6, 2, 8, 2), ("x", "zlo", "zhi", "y", "core"))
    dp, space = ("x", "zlo"), ("zhi", "y", "core")
    specs = (P(dp, space, None), P(dp, space, None), P(dp, None), P(dp, None), P(dp, None))

    return jax.shard_map(body, mesh=fine, in_specs=specs, out_specs=specs, check_vma=False)
```

```python
import jax
import jax.numpy as jnp
from jax import lax
from jax.experimental import pallas as pl
from jax.experimental.pallas import tpu as pltpu
from jax.sharding import Mesh
from jax.sharding import PartitionSpec as P


beta_one = 0.9
beta_two = 0.999
learn_rate = 0.01
decay_rate = 0.01
epsilon = 1e-08
adam_step = 10

C = 160
COUNT = 98304
F32 = jnp.float32
BF16 = jnp.bfloat16
VM = pl.BlockSpec(memory_space=pltpu.VMEM)

PIECE = 40
GRAD_ROWS = 6 * PIECE
SEND_ONE = GRAD_ROWS + 32
SEND_TWO = PIECE + 80


def call(kernel, outs, scratch=(), ins=None, limit=16):
    one = not isinstance(outs, list)
    more = {} if ins is None else {"in_specs": ins}
    return pl.pallas_call(
        kernel,
        **more,
        out_shape=outs,
        out_specs=VM if one else [VM] * len(outs),
        scratch_shapes=list(scratch),
        compiler_params=pltpu.CompilerParams(vmem_limit_bytes=limit << 20),
    )


def tile_rows(piece, wide, groups):
    tiles = []
    for g in range(groups):
        block = piece(wide, g)
        tiles += [block[:, 160 * k : 160 * k + 160] for k in range(4)]
    return tiles


def read_block(ref, g):
    return ref[:, 640 * g : 640 * g + 640].astype(F32)


def pack(rows):
    tail = rows[:, 128:160]
    side = jnp.concatenate([tail[8 * b : 8 * b + 8] for b in range(4)], axis=1)
    return jnp.concatenate([rows[:, 0:128], side], axis=0)


def unpack(piece):
    side = piece[32:40]
    tail = jnp.concatenate([side[:, 32 * b : 32 * b + 32] for b in range(4)], axis=0)
    return jnp.concatenate([piece[0:32], tail], axis=1)


def prepare_kernel(
    image_hbm, cotan_hbm, weight_hbm,
    even_ref, odd_ref, cotan_ref, rows_ref,
    image_ref, own_ref, weight_ref, done,
):
    reads = [
        pltpu.make_async_copy(image_hbm, image_ref, done.at[0]),
        pltpu.make_async_copy(cotan_hbm, cotan_ref, done.at[1]),
        pltpu.make_async_copy(weight_hbm, own_ref, done.at[2]),
    ]
    for read in reads:
        read.start()
    for read in reads:
        read.wait()
    tiles = tile_rows(read_block, image_ref, 16)
    even_ref[...] = jnp.concatenate(tiles[0::2], axis=0).astype(BF16)
    odd_ref[...] = jnp.concatenate(tiles[1::2], axis=0).astype(BF16)
    weight_ref[0:60] = own_ref[...]
    weight_ref[60:64] = jnp.zeros((4, C), F32)
    quarter = 2 * lax.axis_index("core") + lax.axis_index("zhi")
    mine = weight_ref[0:16]
    for q in range(1, 4):
        mine = jnp.where(quarter == q, weight_ref[15 * q : 15 * q + 16], mine)
    tail = mine[:, 128:160]
    lane = lax.broadcasted_iota(jnp.int32, (16, 128), 1) // 32
    tail = jnp.where(lane == lax.axis_index("x"), jnp.concatenate([tail] * 4, axis=1), 0.0)
    rows_ref[...] = jnp.concatenate([mine[:, 0:128], tail], axis=0).astype(BF16)


def grad_kernel(
    even_ref, odd_ref, cotan_ref, rows_ref, below_ref,
    send_ref, taps_ref,
    five_ref, spread_ref, sums_ref,
):
    even = even_ref[...]
    odd = odd_ref[...]
    five_ref[...] = jnp.zeros_like(five_ref)
    five_ref[0:4] = cotan_ref[...].astype(F32)
    five_ref[4:5] = below_ref[0:1].astype(F32)
    out_row = lax.broadcasted_iota(jnp.int32, (24, 8), 0)
    in_row = lax.broadcasted_iota(jnp.int32, (24, 8), 1)
    pick = (2 * in_row + out_row // 8 - 1 == out_row % 8).astype(F32).astype(BF16)
    spread_ref[...] = jnp.dot(pick, five_ref[...].astype(BF16), preferred_element_type=F32)
    taps = []
    for r in range(3):
        cols = tile_rows(lambda ref, g: ref[8 * r : 8 * r + 8, 640 * g : 640 * g + 640], spread_ref, 8)
        block = jnp.concatenate(cols, axis=0).astype(BF16)
        taps_ref[r] = block
        taps.append(block)
    zeros = jnp.zeros((8, C), BF16)

    def put(r, s, left, right):
        row = (3 * r + s) * C
        sums_ref[row : row + C] = lax.dot_general(
            left, right, (((0,), (0,)), ((), ())), preferred_element_type=F32
        )

    for r in range(3):
        put(r, 1, even, taps[r])
        put(r, 2, odd, taps[r])
        put(r, 0, odd[0:248], taps[r][8:256])
    sums_ref[1440:1448] = zeros.astype(F32)
    for x in range(4):
        for core in range(2):
            for low in range(6):
                start = 30 * (2 * (6 * x + low) + core)
                piece = pack(sums_ref[start : start + 32])
                send_ref[2 * x + core, PIECE * low : PIECE * low + PIECE] = piece.astype(BF16)
    for n in range(8):
        send_ref[n, GRAD_ROWS:SEND_ONE] = rows_ref[...]


def decay_kernel(weight_ref, one_ref, two_ref, kept_ref, kept_one_ref, kept_two_ref):
    kept_ref[...] = weight_ref[...] - learn_rate * decay_rate * weight_ref[...]
    kept_one_ref[...] = beta_one * one_ref[...]
    kept_two_ref[...] = beta_two * two_ref[...]


def first_sum_kernel(got_ref, send_ref):
    total = got_ref[0, 0:GRAD_ROWS].astype(F32)
    for n in range(1, 8):
        total = total + got_ref[n, 0:GRAD_ROWS].astype(F32)
    total = total.astype(BF16)
    core = lax.axis_index("core")
    heads = [got_ref[2 * x + core, GRAD_ROWS : GRAD_ROWS + 16] for x in range(4)]
    tail = got_ref[core, GRAD_ROWS + 16 : SEND_ONE].astype(F32)
    for x in range(1, 4):
        tail = tail + got_ref[2 * x + core, GRAD_ROWS + 16 : SEND_ONE].astype(F32)
    tail = tail.astype(BF16)
    for low in range(6):
        for high in range(2):
            n = 2 * low + high
            send_ref[n, 0:PIECE] = total[PIECE * low : PIECE * low + PIECE]
            for x in range(4):
                send_ref[n, PIECE + 16 * x : PIECE + 16 * x + 16] = heads[x]
            send_ref[n, PIECE + 64 : SEND_TWO] = tail


def second_sum_kernel(got_ref, send_ref):
    total = got_ref[0, 0:PIECE].astype(F32)
    for n in range(1, 12):
        total = total + got_ref[n, 0:PIECE].astype(F32)
    total = total.astype(BF16)
    for n in range(16):
        send_ref[n] = total


def conv_kernel(
    image_ref, above_ref, even_ref, odd_ref, taps_ref, own_ref, other_ref,
    out_ref, grad_ref,
    kernel_ref, shift_ref, roll_ref,
):
    core = lax.axis_index("core")
    for x in range(4):
        for low in range(6):
            for c in range(2):
                for high in range(2):
                    n = 2 * low + high
                    own = own_ref[n, PIECE:SEND_TWO].astype(F32)
                    other = other_ref[n, PIECE:SEND_TWO].astype(F32)
                    block = jnp.where(core == c, own, other)
                    start = 60 * (6 * x + low) + 15 * (2 * c + high)
                    kernel_ref[start : start + 16] = jnp.concatenate(
                        [block[16 * x : 16 * x + 16], block[64:80, 32 * x : 32 * x + 32]], axis=1
                    )

    def tap(r, s):
        row = (3 * r + s) * C
        return kernel_ref[row : row + C].astype(BF16)

    def dot(left, right):
        return jnp.dot(left, right, preferred_element_type=F32)

    def dot_t(left, right):
        return lax.dot_general(left, right, (((1,), (1,)), ((), ())), preferred_element_type=F32)

    zeros = jnp.zeros((8, C), BF16)
    even = even_ref[...]
    odd = odd_ref[...]
    odd_before = jnp.concatenate([zeros, odd[0:248]], axis=0)
    shift_ref[0:1] = above_ref[...].astype(F32)
    shift_ref[1:9] = image_ref[...].astype(F32)
    tiles = tile_rows(lambda ref, g: ref[0:8, 640 * g : 640 * g + 640], shift_ref, 16)
    even_down = jnp.concatenate(tiles[0::2], axis=0).astype(BF16)
    odd_down = jnp.concatenate(tiles[1::2], axis=0).astype(BF16)
    odd_down_before = jnp.concatenate([zeros, odd_down[0:248]], axis=0)
    roll_ref[0:256] = dot(even, tap(2, 1)) + dot(odd, tap(2, 2)) + dot(odd_before, tap(2, 0))
    roll_ref[256:264] = jnp.zeros((8, C), F32)
    total = dot(even_down, tap(0, 1)) + dot(odd_down, tap(0, 2)) + dot(odd_down_before, tap(0, 0))
    total = total + dot(even, tap(1, 1)) + dot(odd, tap(1, 2)) + dot(odd_before, tap(1, 0))
    total = total + roll_ref[1:257]
    for g in range(8):
        wide = jnp.concatenate(
            [total[32 * g + 8 * k : 32 * g + 8 * k + 8] for k in range(4)], axis=1
        )
        rows = jnp.concatenate([wide[2 * i : 2 * i + 1] for i in range(4)], axis=0)
        out_ref[:, 640 * g : 640 * g + 640] = rows.astype(BF16)
    taps = [taps_ref[r] for r in range(3)]
    after = [jnp.concatenate([t[8:256], zeros], axis=0) for t in taps]
    grad_even = dot_t(taps[0], tap(0, 1)) + dot_t(taps[1], tap(1, 1)) + dot_t(taps[2], tap(2, 1))
    grad_odd = dot_t(taps[0], tap(0, 2)) + dot_t(taps[1], tap(1, 2)) + dot_t(taps[2], tap(2, 2))
    for r in range(3):
        grad_odd = grad_odd + dot_t(after[r], tap(r, 0))
    for g in range(16):
        parts = []
        for k in range(2):
            row = 16 * g + 8 * k
            parts += [grad_even[row : row + 8], grad_odd[row : row + 8]]
        grad_ref[:, 640 * g : 640 * g + 640] = jnp.concatenate(parts, axis=1).astype(BF16)


def adam_kernel(got_ref, weight_ref, one_ref, two_ref, new_weight_ref, new_one_ref, new_two_ref, sums_ref):
    for core in range(2):
        total = got_ref[core].astype(F32)
        for y in range(1, 8):
            total = total + got_ref[2 * y + core].astype(F32)
        sums_ref[30 * core : 30 * core + 32] = unpack(total)
    gradient = sums_ref[0:60] / float(COUNT)
    new_one = one_ref[...] + (1.0 - beta_one) * gradient
    new_two = two_ref[...] + (1.0 - beta_two) * gradient * gradient
    first_hat = new_one / (1.0 - beta_one**adam_step)
    second_hat = new_two / (1.0 - beta_two**adam_step)
    new_weight_ref[...] = weight_ref[...] - learn_rate * (
        first_hat / (jnp.sqrt(second_hat) + epsilon)
    )
    new_one_ref[...] = new_one
    new_two_ref[...] = new_two


def from_behind(block, distance):
    axes = ("zhi", "y", "core")
    route = [(i - distance, i) for i in range(32) if 0 <= i - distance < 32]
    return lax.ppermute(block, axes, route)


def body(image, cotangent, weight, moment_one, moment_two):
    shape = jax.ShapeDtypeStruct
    image = image.reshape(8, 64 * C)
    cotangent = cotangent.reshape(4, 32 * C)
    below = from_behind(cotangent, -1)
    even, odd, strip, rows = call(
        prepare_kernel,
        [
            shape((256, C), BF16),
            shape((256, C), BF16),
            shape((4, 32 * C), BF16),
            shape((32, 128), BF16),
        ],
        [
            pltpu.VMEM((8, 64 * C), BF16),
            pltpu.VMEM((60, C), F32),
            pltpu.VMEM((64, C), F32),
            pltpu.SemaphoreType.DMA((3,)),
        ],
        [pl.BlockSpec(memory_space=pltpu.HBM)] * 3,
    )(*[pltpu.with_memory_space_constraint(a, pltpu.HBM) for a in (image, cotangent, weight)])
    send_one, taps = call(
        grad_kernel,
        [shape((8, SEND_ONE, 128), BF16), shape((3, 256, C), BF16)],
        [
            pltpu.VMEM((8, 32 * C), F32),
            pltpu.VMEM((24, 32 * C), F32),
            pltpu.VMEM((1448, C), F32),
        ],
    )(even, odd, strip, rows, below)
    got_one = lax.all_to_all(send_one, ("x", "core"), 0, 0, tiled=True)
    above = from_behind(image[7:8], 1)
    kept = call(decay_kernel, [shape((60, C), F32)] * 3)(weight, moment_one, moment_two)
    send_two = call(first_sum_kernel, shape((12, SEND_TWO, 128), BF16))(got_one)
    got_two = lax.all_to_all(send_two, ("zlo", "zhi"), 0, 0, tiled=True)
    other = lax.ppermute(got_two, "core", [(0, 1), (1, 0)])
    send_three = call(second_sum_kernel, shape((16, PIECE, 128), BF16))(got_two)
    got_three = lax.all_to_all(send_three, ("y", "core"), 0, 0, tiled=True)
    output, grad_image = call(
        conv_kernel,
        [shape((4, 32 * C), BF16), shape((8, 64 * C), BF16)],
        [
            pltpu.VMEM((1448, C), F32),
            pltpu.VMEM((16, 64 * C), F32),
            pltpu.VMEM((264, C), F32),
        ],
    )(image, above, even, odd, taps, got_two, other)
    new_weight, new_one, new_two = call(
        adam_kernel, [shape((60, C), F32)] * 3, [pltpu.VMEM((64, C), F32)]
    )(got_three, *kept)
    return (output[None], grad_image[None], new_weight, new_one, new_two)


def solution(mesh):
    fine = Mesh(mesh.devices.reshape(4, 6, 2, 8, 2), ("x", "zlo", "zhi", "y", "core"))
    dp, space = ("x", "zlo"), ("zhi", "y", "core")
    specs = (P(dp, space, None), P(dp, space, None), P(dp, None), P(dp, None), P(dp, None))

    return jax.shard_map(body, mesh=fine, in_specs=specs, out_specs=specs, check_vma=False)
```

```python
import jax
import jax.numpy as jnp
from jax import lax
from jax.experimental import pallas as pl
from jax.experimental.pallas import tpu as pltpu
from jax.sharding import Mesh
from jax.sharding import PartitionSpec as P


beta_one = 0.9
beta_two = 0.999
learn_rate = 0.01
decay_rate = 0.01
epsilon = 1e-08
adam_step = 10

C = 160
COUNT = 98304
F32 = jnp.float32
BF16 = jnp.bfloat16
VM = pl.BlockSpec(memory_space=pltpu.VMEM)

PIECE = 40
GRAD_ROWS = 6 * PIECE
SEND_ONE = GRAD_ROWS + 32
SEND_TWO = PIECE + 80


def call(kernel, outs, scratch=(), ins=None, limit=16):
    one = not isinstance(outs, list)
    more = {} if ins is None else {"in_specs": ins}
    return pl.pallas_call(
        kernel,
        **more,
        out_shape=outs,
        out_specs=VM if one else [VM] * len(outs),
        scratch_shapes=list(scratch),
        compiler_params=pltpu.CompilerParams(vmem_limit_bytes=limit << 20),
    )


def tile_rows(piece, wide, groups):
    tiles = []
    for g in range(groups):
        block = piece(wide, g)
        tiles += [block[:, 160 * k : 160 * k + 160] for k in range(4)]
    return tiles


def read_block(ref, g):
    return ref[:, 640 * g : 640 * g + 640].astype(F32)


def pack(rows):
    tail = rows[:, 128:160]
    side = jnp.concatenate([tail[8 * b : 8 * b + 8] for b in range(4)], axis=1)
    return jnp.concatenate([rows[:, 0:128], side], axis=0)


def unpack(piece):
    side = piece[32:40]
    tail = jnp.concatenate([side[:, 32 * b : 32 * b + 32] for b in range(4)], axis=0)
    return jnp.concatenate([piece[0:32], tail], axis=1)


def prepare_kernel(
    image_hbm, cotan_hbm, weight_hbm,
    even_ref, odd_ref, cotan_ref, rows_ref,
    image_ref, own_ref, weight_ref, done,
):
    reads = [
        pltpu.make_async_copy(image_hbm, image_ref, done.at[0]),
        pltpu.make_async_copy(cotan_hbm, cotan_ref, done.at[1]),
        pltpu.make_async_copy(weight_hbm, own_ref, done.at[2]),
    ]
    for read in reads:
        read.start()
    for read in reads:
        read.wait()
    tiles = tile_rows(read_block, image_ref, 16)
    even_ref[...] = jnp.concatenate(tiles[0::2], axis=0).astype(BF16)
    odd_ref[...] = jnp.concatenate(tiles[1::2], axis=0).astype(BF16)
    weight_ref[0:60] = own_ref[...]
    weight_ref[60:64] = jnp.zeros((4, C), F32)
    quarter = 2 * lax.axis_index("core") + lax.axis_index("zhi")
    mine = weight_ref[0:16]
    for q in range(1, 4):
        mine = jnp.where(quarter == q, weight_ref[15 * q : 15 * q + 16], mine)
    tail = mine[:, 128:160]
    lane = lax.broadcasted_iota(jnp.int32, (16, 128), 1) // 32
    tail = jnp.where(lane == lax.axis_index("x"), jnp.concatenate([tail] * 4, axis=1), 0.0)
    rows_ref[...] = jnp.concatenate([mine[:, 0:128], tail], axis=0).astype(BF16)


def grad_kernel(
    even_ref, odd_ref, cotan_ref, below_ref,
    keep_ref, give_ref, taps_ref,
    five_ref, spread_ref, sums_ref,
):
    even = even_ref[...]
    odd = odd_ref[...]
    five_ref[...] = jnp.zeros_like(five_ref)
    five_ref[0:4] = cotan_ref[...].astype(F32)
    five_ref[4:5] = below_ref[0:1].astype(F32)
    out_row = lax.broadcasted_iota(jnp.int32, (24, 8), 0)
    in_row = lax.broadcasted_iota(jnp.int32, (24, 8), 1)
    pick = (2 * in_row + out_row // 8 - 1 == out_row % 8).astype(F32).astype(BF16)
    spread_ref[...] = jnp.dot(pick, five_ref[...].astype(BF16), preferred_element_type=F32)
    taps = []
    for r in range(3):
        cols = tile_rows(lambda ref, g: ref[8 * r : 8 * r + 8, 640 * g : 640 * g + 640], spread_ref, 8)
        block = jnp.concatenate(cols, axis=0).astype(BF16)
        taps_ref[r] = block
        taps.append(block)
    zeros = jnp.zeros((8, C), BF16)

    def put(r, s, left, right):
        row = (3 * r + s) * C
        sums_ref[row : row + C] = lax.dot_general(
            left, right, (((0,), (0,)), ((), ())), preferred_element_type=F32
        )

    for r in range(3):
        put(r, 1, even, taps[r])
        put(r, 2, odd, taps[r])
        put(r, 0, odd[0:248], taps[r][8:256])
    sums_ref[1440:1448] = zeros.astype(F32)
    first = lax.axis_index("core") == 0
    for x in range(4):
        for low in range(6):
            start = 60 * (6 * x + low)
            halves = [pack(sums_ref[start + 30 * c : start + 30 * c + 32]) for c in range(2)]
            at = slice(PIECE * low, PIECE * low + PIECE)
            keep_ref[x, at] = jnp.where(first, halves[0], halves[1]).astype(BF16)
            give_ref[x, at] = jnp.where(first, halves[1], halves[0]).astype(BF16)


def core_sum_kernel(keep_ref, got_ref, rows_ref, send_ref):
    for x in range(4):
        total = keep_ref[x].astype(F32) + got_ref[x].astype(F32)
        send_ref[x, 0:GRAD_ROWS] = total.astype(BF16)
        send_ref[x, GRAD_ROWS:SEND_ONE] = rows_ref[...]


def decay_kernel(weight_ref, one_ref, two_ref, kept_ref, kept_one_ref, kept_two_ref):
    kept_ref[...] = weight_ref[...] - learn_rate * decay_rate * weight_ref[...]
    kept_one_ref[...] = beta_one * one_ref[...]
    kept_two_ref[...] = beta_two * two_ref[...]


def first_sum_kernel(got_ref, send_ref):
    total = got_ref[0, 0:GRAD_ROWS].astype(F32)
    tail = got_ref[0, GRAD_ROWS + 16 : SEND_ONE].astype(F32)
    for x in range(1, 4):
        total = total + got_ref[x, 0:GRAD_ROWS].astype(F32)
        tail = tail + got_ref[x, GRAD_ROWS + 16 : SEND_ONE].astype(F32)
    total = total.astype(BF16)
    tail = tail.astype(BF16)
    heads = [got_ref[x, GRAD_ROWS : GRAD_ROWS + 16] for x in range(4)]
    for low in range(6):
        for high in range(2):
            n = 2 * low + high
            send_ref[n, 0:PIECE] = total[PIECE * low : PIECE * low + PIECE]
            for x in range(4):
                send_ref[n, PIECE + 16 * x : PIECE + 16 * x + 16] = heads[x]
            send_ref[n, PIECE + 64 : SEND_TWO] = tail


def second_sum_kernel(got_ref, send_ref):
    total = got_ref[0, 0:PIECE].astype(F32)
    for n in range(1, 12):
        total = total + got_ref[n, 0:PIECE].astype(F32)
    total = total.astype(BF16)
    for n in range(16):
        send_ref[n] = total


def conv_kernel(
    image_ref, above_ref, even_ref, odd_ref, taps_ref, own_ref, other_ref,
    out_ref, grad_ref,
    kernel_ref, shift_ref, roll_ref,
):
    core = lax.axis_index("core")
    for x in range(4):
        for low in range(6):
            for c in range(2):
                for high in range(2):
                    n = 2 * low + high
                    own = own_ref[n, PIECE:SEND_TWO].astype(F32)
                    other = other_ref[n, PIECE:SEND_TWO].astype(F32)
                    block = jnp.where(core == c, own, other)
                    start = 60 * (6 * x + low) + 15 * (2 * c + high)
                    kernel_ref[start : start + 16] = jnp.concatenate(
                        [block[16 * x : 16 * x + 16], block[64:80, 32 * x : 32 * x + 32]], axis=1
                    )

    def tap(r, s):
        row = (3 * r + s) * C
        return kernel_ref[row : row + C].astype(BF16)

    def dot(left, right):
        return jnp.dot(left, right, preferred_element_type=F32)

    def dot_t(left, right):
        return lax.dot_general(left, right, (((1,), (1,)), ((), ())), preferred_element_type=F32)

    zeros = jnp.zeros((8, C), BF16)
    even = even_ref[...]
    odd = odd_ref[...]
    odd_before = jnp.concatenate([zeros, odd[0:248]], axis=0)
    shift_ref[0:1] = above_ref[...].astype(F32)
    shift_ref[1:9] = image_ref[...].astype(F32)
    tiles = tile_rows(lambda ref, g: ref[0:8, 640 * g : 640 * g + 640], shift_ref, 16)
    even_down = jnp.concatenate(tiles[0::2], axis=0).astype(BF16)
    odd_down = jnp.concatenate(tiles[1::2], axis=0).astype(BF16)
    odd_down_before = jnp.concatenate([zeros, odd_down[0:248]], axis=0)
    roll_ref[0:256] = dot(even, tap(2, 1)) + dot(odd, tap(2, 2)) + dot(odd_before, tap(2, 0))
    roll_ref[256:264] = jnp.zeros((8, C), F32)
    total = dot(even_down, tap(0, 1)) + dot(odd_down, tap(0, 2)) + dot(odd_down_before, tap(0, 0))
    total = total + dot(even, tap(1, 1)) + dot(odd, tap(1, 2)) + dot(odd_before, tap(1, 0))
    total = total + roll_ref[1:257]
    for g in range(8):
        wide = jnp.concatenate(
            [total[32 * g + 8 * k : 32 * g + 8 * k + 8] for k in range(4)], axis=1
        )
        rows = jnp.concatenate([wide[2 * i : 2 * i + 1] for i in range(4)], axis=0)
        out_ref[:, 640 * g : 640 * g + 640] = rows.astype(BF16)
    taps = [taps_ref[r] for r in range(3)]
    after = [jnp.concatenate([t[8:256], zeros], axis=0) for t in taps]
    grad_even = dot_t(taps[0], tap(0, 1)) + dot_t(taps[1], tap(1, 1)) + dot_t(taps[2], tap(2, 1))
    grad_odd = dot_t(taps[0], tap(0, 2)) + dot_t(taps[1], tap(1, 2)) + dot_t(taps[2], tap(2, 2))
    for r in range(3):
        grad_odd = grad_odd + dot_t(after[r], tap(r, 0))
    for g in range(16):
        parts = []
        for k in range(2):
            row = 16 * g + 8 * k
            parts += [grad_even[row : row + 8], grad_odd[row : row + 8]]
        grad_ref[:, 640 * g : 640 * g + 640] = jnp.concatenate(parts, axis=1).astype(BF16)


def adam_kernel(got_ref, weight_ref, one_ref, two_ref, new_weight_ref, new_one_ref, new_two_ref, sums_ref):
    for core in range(2):
        total = got_ref[core].astype(F32)
        for y in range(1, 8):
            total = total + got_ref[2 * y + core].astype(F32)
        sums_ref[30 * core : 30 * core + 32] = unpack(total)
    gradient = sums_ref[0:60] / float(COUNT)
    new_one = one_ref[...] + (1.0 - beta_one) * gradient
    new_two = two_ref[...] + (1.0 - beta_two) * gradient * gradient
    first_hat = new_one / (1.0 - beta_one**adam_step)
    second_hat = new_two / (1.0 - beta_two**adam_step)
    new_weight_ref[...] = weight_ref[...] - learn_rate * (
        first_hat / (jnp.sqrt(second_hat) + epsilon)
    )
    new_one_ref[...] = new_one
    new_two_ref[...] = new_two


def from_behind(block, distance):
    axes = ("zhi", "y", "core")
    route = [(i - distance, i) for i in range(32) if 0 <= i - distance < 32]
    return lax.ppermute(block, axes, route)


def body(image, cotangent, weight, moment_one, moment_two):
    shape = jax.ShapeDtypeStruct
    image = image.reshape(8, 64 * C)
    cotangent = cotangent.reshape(4, 32 * C)
    below = from_behind(cotangent, -1)
    even, odd, strip, rows = call(
        prepare_kernel,
        [
            shape((256, C), BF16),
            shape((256, C), BF16),
            shape((4, 32 * C), BF16),
            shape((32, 128), BF16),
        ],
        [
            pltpu.VMEM((8, 64 * C), BF16),
            pltpu.VMEM((60, C), F32),
            pltpu.VMEM((64, C), F32),
            pltpu.SemaphoreType.DMA((3,)),
        ],
        [pl.BlockSpec(memory_space=pltpu.HBM)] * 3,
    )(*[pltpu.with_memory_space_constraint(a, pltpu.HBM) for a in (image, cotangent, weight)])
    keep, give, taps = call(
        grad_kernel,
        [shape((4, GRAD_ROWS, 128), BF16)] * 2 + [shape((3, 256, C), BF16)],
        [
            pltpu.VMEM((8, 32 * C), F32),
            pltpu.VMEM((24, 32 * C), F32),
            pltpu.VMEM((1448, C), F32),
        ],
    )(even, odd, strip, below)
    given = lax.ppermute(give, "core", [(0, 1), (1, 0)])
    send_one = call(core_sum_kernel, shape((4, SEND_ONE, 128), BF16))(keep, given, rows)
    got_one = lax.all_to_all(send_one, "x", 0, 0, tiled=True)
    above = from_behind(image[7:8], 1)
    kept = call(decay_kernel, [shape((60, C), F32)] * 3)(weight, moment_one, moment_two)
    send_two = call(first_sum_kernel, shape((12, SEND_TWO, 128), BF16))(got_one)
    got_two = lax.all_to_all(send_two, ("zlo", "zhi"), 0, 0, tiled=True)
    other = lax.ppermute(got_two, "core", [(0, 1), (1, 0)])
    send_three = call(second_sum_kernel, shape((16, PIECE, 128), BF16))(got_two)
    got_three = lax.all_to_all(send_three, ("y", "core"), 0, 0, tiled=True)
    output, grad_image = call(
        conv_kernel,
        [shape((4, 32 * C), BF16), shape((8, 64 * C), BF16)],
        [
            pltpu.VMEM((1448, C), F32),
            pltpu.VMEM((16, 64 * C), F32),
            pltpu.VMEM((264, C), F32),
        ],
    )(image, above, even, odd, taps, got_two, other)
    new_weight, new_one, new_two = call(
        adam_kernel, [shape((60, C), F32)] * 3, [pltpu.VMEM((64, C), F32)]
    )(got_three, *kept)
    return (output[None], grad_image[None], new_weight, new_one, new_two)


def solution(mesh):
    fine = Mesh(mesh.devices.reshape(4, 6, 2, 8, 2), ("x", "zlo", "zhi", "y", "core"))
    dp, space = ("x", "zlo"), ("zhi", "y", "core")
    specs = (P(dp, space, None), P(dp, space, None), P(dp, None), P(dp, None), P(dp, None))

    return jax.shard_map(body, mesh=fine, in_specs=specs, out_specs=specs, check_vma=False)
```

```python
import jax
import jax.numpy as jnp
from jax import lax
from jax.experimental import pallas as pl
from jax.experimental.pallas import tpu as pltpu
from jax.sharding import Mesh
from jax.sharding import PartitionSpec as P


beta_one = 0.9
beta_two = 0.999
learn_rate = 0.01
decay_rate = 0.01
epsilon = 1e-08
adam_step = 10

C = 160
COUNT = 98304
F32 = jnp.float32
BF16 = jnp.bfloat16
VM = pl.BlockSpec(memory_space=pltpu.VMEM)

PIECE = 40
GRAD_ROWS = 6 * PIECE
SEND_ONE = GRAD_ROWS + 32
SEND_TWO = PIECE + 80
SWAP_ROWS = GRAD_ROWS + PIECE


def call(kernel, outs, scratch=(), ins=None, limit=16):
    one = not isinstance(outs, list)
    more = {} if ins is None else {"in_specs": ins}
    return pl.pallas_call(
        kernel,
        **more,
        out_shape=outs,
        out_specs=VM if one else [VM] * len(outs),
        scratch_shapes=list(scratch),
        compiler_params=pltpu.CompilerParams(vmem_limit_bytes=limit << 20),
    )


def tile_rows(piece, wide, groups):
    tiles = []
    for g in range(groups):
        block = piece(wide, g)
        tiles += [block[:, 160 * k : 160 * k + 160] for k in range(4)]
    return tiles


def read_block(ref, g):
    return ref[:, 640 * g : 640 * g + 640].astype(F32)


def every(offset, across=False):
    shape, short, long = ((256, 32), 1, 0) if across else ((32, 256), 0, 1)
    hit = lax.broadcasted_iota(jnp.int32, shape, long) == 8 * lax.broadcasted_iota(
        jnp.int32, shape, short
    ) + offset
    return hit.astype(F32).astype(BF16)


def pack(rows):
    tail = rows[:, 128:160]
    side = jnp.concatenate([tail[8 * b : 8 * b + 8] for b in range(4)], axis=1)
    return jnp.concatenate([rows[:, 0:128], side], axis=0)


def unpack(piece):
    side = piece[32:40]
    tail = jnp.concatenate([side[:, 32 * b : 32 * b + 32] for b in range(4)], axis=0)
    return jnp.concatenate([piece[0:32], tail], axis=1)


def prepare_kernel(
    image_hbm, cotan_hbm, weight_hbm,
    even_ref, odd_ref, cotan_ref, rows_ref, edge_ref,
    image_ref, own_ref, weight_ref, done,
):
    reads = [
        pltpu.make_async_copy(image_hbm, image_ref, done.at[0]),
        pltpu.make_async_copy(cotan_hbm, cotan_ref, done.at[1]),
        pltpu.make_async_copy(weight_hbm, own_ref, done.at[2]),
    ]
    for read in reads:
        read.start()
    for read in reads:
        read.wait()
    tiles = tile_rows(read_block, image_ref, 16)
    even = jnp.concatenate(tiles[0::2], axis=0).astype(BF16)
    odd = jnp.concatenate(tiles[1::2], axis=0).astype(BF16)
    even_ref[...] = even
    odd_ref[...] = odd
    edge_ref[0] = jnp.dot(every(7), even, preferred_element_type=F32).astype(BF16)
    edge_ref[1] = jnp.dot(every(7), odd, preferred_element_type=F32).astype(BF16)
    weight_ref[0:60] = own_ref[...]
    weight_ref[60:64] = jnp.zeros((4, C), F32)
    quarter = 2 * lax.axis_index("core") + lax.axis_index("zhi")
    mine = weight_ref[0:16]
    for q in range(1, 4):
        mine = jnp.where(quarter == q, weight_ref[15 * q : 15 * q + 16], mine)
    tail = mine[:, 128:160]
    lane = lax.broadcasted_iota(jnp.int32, (16, 128), 1) // 32
    tail = jnp.where(lane == lax.axis_index("x"), jnp.concatenate([tail] * 4, axis=1), 0.0)
    rows_ref[...] = jnp.concatenate([mine[:, 0:128], tail], axis=0).astype(BF16)


def grad_kernel(
    even_ref, odd_ref, cotan_ref, edge_ref,
    keep_ref, give_ref, taps_ref, first_ref,
    five_ref, spread_ref, sums_ref,
):
    even = even_ref[...]
    odd = odd_ref[...]
    five_ref[...] = jnp.zeros_like(five_ref)
    five_ref[0:4] = cotan_ref[...].astype(F32)
    out_row = lax.broadcasted_iota(jnp.int32, (24, 8), 0)
    in_row = lax.broadcasted_iota(jnp.int32, (24, 8), 1)
    pick = (2 * in_row + out_row // 8 - 1 == out_row % 8).astype(F32).astype(BF16)
    spread_ref[...] = jnp.dot(pick, five_ref[...].astype(BF16), preferred_element_type=F32)
    taps = []
    for r in range(3):
        cols = tile_rows(lambda ref, g: ref[8 * r : 8 * r + 8, 640 * g : 640 * g + 640], spread_ref, 8)
        block = jnp.concatenate(cols, axis=0).astype(BF16)
        taps_ref[r] = block
        taps.append(block)
    zeros = jnp.zeros((8, C), BF16)

    def put(r, s, left, right):
        row = (3 * r + s) * C
        sums_ref[row : row + C] = lax.dot_general(
            left, right, (((0,), (0,)), ((), ())), preferred_element_type=F32
        )

    for r in range(3):
        put(r, 1, even, taps[r])
        put(r, 2, odd, taps[r])
        put(r, 0, odd[0:248], taps[r][8:256])
    sums_ref[1440:1448] = zeros.astype(F32)
    first = lax.axis_index("core") == 0
    for x in range(4):
        for low in range(6):
            start = 60 * (6 * x + low)
            halves = [pack(sums_ref[start + 30 * c : start + 30 * c + 32]) for c in range(2)]
            at = slice(PIECE * low, PIECE * low + PIECE)
            keep_ref[x, at] = jnp.where(first, halves[0], halves[1]).astype(BF16)
            give_ref[x, at] = jnp.where(first, halves[1], halves[0]).astype(BF16)
    top = jnp.dot(every(0), taps[1], preferred_element_type=F32)
    first_ref[...] = top.astype(BF16)
    edges = [edge_ref[0].astype(F32), edge_ref[1].astype(F32), top, jnp.zeros_like(top)]
    for k in range(4):
        give_ref[k, GRAD_ROWS:SWAP_ROWS] = pack(edges[k]).astype(BF16)


def core_sum_kernel(
    keep_ref, got_ref, rows_ref, edge_ref, first_ref, next_zero_ref, next_one_ref,
    send_ref, below_ref,
    edge_sum_ref,
):
    first = lax.axis_index("core") == 0

    def other(k):
        return unpack(got_ref[k, GRAD_ROWS:SWAP_ROWS].astype(F32))

    def both(k):
        mine, yours = edge_ref[k].astype(F32), other(k)
        pair = [jnp.where(first, mine, yours), jnp.where(first, yours, mine)]
        return jnp.concatenate(pair, axis=0).astype(BF16)

    inner = jnp.where(first, other(2), first_ref[...].astype(F32))
    flat = next_zero_ref[...].astype(F32) + next_one_ref[...].astype(F32)
    outer = jnp.concatenate([flat[0:1, C * j : C * j + C] for j in range(32)], axis=0)
    below_ref[...] = jnp.where(first, inner, outer).astype(BF16)
    zero = jnp.zeros((1, C), F32)
    rights = [
        jnp.concatenate([inner[1:32], zero, outer[1:32], zero], axis=0).astype(BF16),
        jnp.concatenate([inner, outer], axis=0).astype(BF16),
    ]
    even, odd = both(0), both(1)
    edge_sum_ref[480:512] = jnp.zeros((32, C), F32)
    for s, left in ((0, odd), (1, even), (2, odd)):
        edge_sum_ref[C * s : C * s + C] = lax.dot_general(
            left, rights[min(s, 1)], (((0,), (0,)), ((), ())), preferred_element_type=F32
        )
    for x in range(4):
        total = keep_ref[x].astype(F32) + got_ref[x, 0:GRAD_ROWS].astype(F32)
        parts = []
        for low in range(6):
            part = total[PIECE * low : PIECE * low + PIECE]
            start = 60 * (6 * x + low)
            if start < 480:
                halves = [edge_sum_ref[start + 30 * c : start + 30 * c + 32] for c in range(2)]
                part = part + pack(jnp.where(first, halves[0], halves[1]))
            parts.append(part)
        send_ref[x, 0:GRAD_ROWS] = jnp.concatenate(parts, axis=0).astype(BF16)
        send_ref[x, GRAD_ROWS:SEND_ONE] = rows_ref[...]


def decay_kernel(weight_ref, one_ref, two_ref, kept_ref, kept_one_ref, kept_two_ref):
    kept_ref[...] = weight_ref[...] - learn_rate * decay_rate * weight_ref[...]
    kept_one_ref[...] = beta_one * one_ref[...]
    kept_two_ref[...] = beta_two * two_ref[...]


def first_sum_kernel(got_ref, send_ref):
    total = got_ref[0, 0:GRAD_ROWS].astype(F32)
    tail = got_ref[0, GRAD_ROWS + 16 : SEND_ONE].astype(F32)
    for x in range(1, 4):
        total = total + got_ref[x, 0:GRAD_ROWS].astype(F32)
        tail = tail + got_ref[x, GRAD_ROWS + 16 : SEND_ONE].astype(F32)
    total = total.astype(BF16)
    tail = tail.astype(BF16)
    heads = [got_ref[x, GRAD_ROWS : GRAD_ROWS + 16] for x in range(4)]
    for low in range(6):
        for high in range(2):
            n = 2 * low + high
            send_ref[n, 0:PIECE] = total[PIECE * low : PIECE * low + PIECE]
            for x in range(4):
                send_ref[n, PIECE + 16 * x : PIECE + 16 * x + 16] = heads[x]
            send_ref[n, PIECE + 64 : SEND_TWO] = tail


def second_sum_kernel(got_ref, send_ref):
    total = got_ref[0, 0:PIECE].astype(F32)
    for n in range(1, 12):
        total = total + got_ref[n, 0:PIECE].astype(F32)
    total = total.astype(BF16)
    for n in range(16):
        send_ref[n] = total


def conv_kernel(
    image_ref, above_ref, even_ref, odd_ref, taps_ref, below_ref, own_ref, other_ref,
    out_ref, grad_ref,
    kernel_ref, shift_ref, roll_ref,
):
    core = lax.axis_index("core")
    for x in range(4):
        for low in range(6):
            for c in range(2):
                for high in range(2):
                    n = 2 * low + high
                    own = own_ref[n, PIECE:SEND_TWO].astype(F32)
                    other = other_ref[n, PIECE:SEND_TWO].astype(F32)
                    block = jnp.where(core == c, own, other)
                    start = 60 * (6 * x + low) + 15 * (2 * c + high)
                    kernel_ref[start : start + 16] = jnp.concatenate(
                        [block[16 * x : 16 * x + 16], block[64:80, 32 * x : 32 * x + 32]], axis=1
                    )

    def tap(r, s):
        row = (3 * r + s) * C
        return kernel_ref[row : row + C].astype(BF16)

    def dot(left, right):
        return jnp.dot(left, right, preferred_element_type=F32)

    def dot_t(left, right):
        return lax.dot_general(left, right, (((1,), (1,)), ((), ())), preferred_element_type=F32)

    zeros = jnp.zeros((8, C), BF16)
    even = even_ref[...]
    odd = odd_ref[...]
    odd_before = jnp.concatenate([zeros, odd[0:248]], axis=0)
    shift_ref[0:1] = above_ref[...].astype(F32)
    shift_ref[1:9] = image_ref[...].astype(F32)
    tiles = tile_rows(lambda ref, g: ref[0:8, 640 * g : 640 * g + 640], shift_ref, 16)
    even_down = jnp.concatenate(tiles[0::2], axis=0).astype(BF16)
    odd_down = jnp.concatenate(tiles[1::2], axis=0).astype(BF16)
    odd_down_before = jnp.concatenate([zeros, odd_down[0:248]], axis=0)
    roll_ref[0:256] = dot(even, tap(2, 1)) + dot(odd, tap(2, 2)) + dot(odd_before, tap(2, 0))
    roll_ref[256:264] = jnp.zeros((8, C), F32)
    total = dot(even_down, tap(0, 1)) + dot(odd_down, tap(0, 2)) + dot(odd_down_before, tap(0, 0))
    total = total + dot(even, tap(1, 1)) + dot(odd, tap(1, 2)) + dot(odd_before, tap(1, 0))
    total = total + roll_ref[1:257]
    for g in range(8):
        wide = jnp.concatenate(
            [total[32 * g + 8 * k : 32 * g + 8 * k + 8] for k in range(4)], axis=1
        )
        rows = jnp.concatenate([wide[2 * i : 2 * i + 1] for i in range(4)], axis=0)
        out_ref[:, 640 * g : 640 * g + 640] = rows.astype(BF16)
    taps = [taps_ref[r] for r in range(3)]
    last = jnp.dot(every(7, True), below_ref[...], preferred_element_type=F32)
    taps[0] = (taps[0].astype(F32) + last).astype(BF16)
    after = [jnp.concatenate([t[8:256], zeros], axis=0) for t in taps]
    grad_even = dot_t(taps[0], tap(0, 1)) + dot_t(taps[1], tap(1, 1)) + dot_t(taps[2], tap(2, 1))
    grad_odd = dot_t(taps[0], tap(0, 2)) + dot_t(taps[1], tap(1, 2)) + dot_t(taps[2], tap(2, 2))
    for r in range(3):
        grad_odd = grad_odd + dot_t(after[r], tap(r, 0))
    for g in range(16):
        parts = []
        for k in range(2):
            row = 16 * g + 8 * k
            parts += [grad_even[row : row + 8], grad_odd[row : row + 8]]
        grad_ref[:, 640 * g : 640 * g + 640] = jnp.concatenate(parts, axis=1).astype(BF16)


def adam_kernel(got_ref, weight_ref, one_ref, two_ref, new_weight_ref, new_one_ref, new_two_ref, sums_ref):
    for core in range(2):
        total = got_ref[core].astype(F32)
        for y in range(1, 8):
            total = total + got_ref[2 * y + core].astype(F32)
        sums_ref[30 * core : 30 * core + 32] = unpack(total)
    gradient = sums_ref[0:60] / float(COUNT)
    new_one = one_ref[...] + (1.0 - beta_one) * gradient
    new_two = two_ref[...] + (1.0 - beta_two) * gradient * gradient
    first_hat = new_one / (1.0 - beta_one**adam_step)
    second_hat = new_two / (1.0 - beta_two**adam_step)
    new_weight_ref[...] = weight_ref[...] - learn_rate * (
        first_hat / (jnp.sqrt(second_hat) + epsilon)
    )
    new_one_ref[...] = new_one
    new_two_ref[...] = new_two


def from_behind(block, distance):
    axes = ("zhi", "y", "core")
    route = [(i - distance, i) for i in range(32) if 0 <= i - distance < 32]
    return lax.ppermute(block, axes, route)


def body(image, cotangent, weight, moment_one, moment_two):
    shape = jax.ShapeDtypeStruct
    image = image.reshape(8, 64 * C)
    cotangent = cotangent.reshape(4, 32 * C)
    axes = ("zhi", "y", "core")
    next_chip = []
    for core in range(2):
        route = [(i, i - 2 + core) for i in range(2, 32, 2)]
        next_chip.append(lax.ppermute(cotangent, axes, route))
    even, odd, strip, rows, edge = call(
        prepare_kernel,
        [
            shape((256, C), BF16),
            shape((256, C), BF16),
            shape((4, 32 * C), BF16),
            shape((32, 128), BF16),
            shape((2, 32, C), BF16),
        ],
        [
            pltpu.VMEM((8, 64 * C), BF16),
            pltpu.VMEM((60, C), F32),
            pltpu.VMEM((64, C), F32),
            pltpu.SemaphoreType.DMA((3,)),
        ],
        [pl.BlockSpec(memory_space=pltpu.HBM)] * 3,
    )(*[pltpu.with_memory_space_constraint(a, pltpu.HBM) for a in (image, cotangent, weight)])
    keep, give, taps, first = call(
        grad_kernel,
        [
            shape((4, GRAD_ROWS, 128), BF16),
            shape((4, SWAP_ROWS, 128), BF16),
            shape((3, 256, C), BF16),
            shape((32, C), BF16),
        ],
        [
            pltpu.VMEM((8, 32 * C), F32),
            pltpu.VMEM((24, 32 * C), F32),
            pltpu.VMEM((1448, C), F32),
        ],
    )(even, odd, strip, edge)
    given = lax.ppermute(give, "core", [(0, 1), (1, 0)])
    send_one, under = call(
        core_sum_kernel,
        [shape((4, SEND_ONE, 128), BF16), shape((32, C), BF16)],
        [pltpu.VMEM((512, C), F32)],
    )(keep, given, rows, edge, first, *next_chip)
    got_one = lax.all_to_all(send_one, "x", 0, 0, tiled=True)
    above = from_behind(image[7:8], 1)
    kept = call(decay_kernel, [shape((60, C), F32)] * 3)(weight, moment_one, moment_two)
    send_two = call(first_sum_kernel, shape((12, SEND_TWO, 128), BF16))(got_one)
    got_two = lax.all_to_all(send_two, ("zlo", "zhi"), 0, 0, tiled=True)
    other = lax.ppermute(got_two, "core", [(0, 1), (1, 0)])
    send_three = call(second_sum_kernel, shape((16, PIECE, 128), BF16))(got_two)
    got_three = lax.all_to_all(send_three, ("y", "core"), 0, 0, tiled=True)
    output, grad_image = call(
        conv_kernel,
        [shape((4, 32 * C), BF16), shape((8, 64 * C), BF16)],
        [
            pltpu.VMEM((1448, C), F32),
            pltpu.VMEM((16, 64 * C), F32),
            pltpu.VMEM((264, C), F32),
        ],
    )(image, above, even, odd, taps, under, got_two, other)
    new_weight, new_one, new_two = call(
        adam_kernel, [shape((60, C), F32)] * 3, [pltpu.VMEM((64, C), F32)]
    )(got_three, *kept)
    return (output[None], grad_image[None], new_weight, new_one, new_two)


def solution(mesh):
    fine = Mesh(mesh.devices.reshape(4, 6, 2, 8, 2), ("x", "zlo", "zhi", "y", "core"))
    dp, space = ("x", "zlo"), ("zhi", "y", "core")
    specs = (P(dp, space, None), P(dp, space, None), P(dp, None), P(dp, None), P(dp, None))

    return jax.shard_map(body, mesh=fine, in_specs=specs, out_specs=specs, check_vma=False)
```

```python
import jax
import jax.numpy as jnp
from jax import lax
from jax.experimental import pallas as pl
from jax.experimental.pallas import tpu as pltpu
from jax.sharding import Mesh
from jax.sharding import PartitionSpec as P


beta_one = 0.9
beta_two = 0.999
learn_rate = 0.01
decay_rate = 0.01
epsilon = 1e-08
adam_step = 10

C = 160
COUNT = 98304
F32 = jnp.float32
BF16 = jnp.bfloat16
VM = pl.BlockSpec(memory_space=pltpu.VMEM)

PIECE = 40
GRAD_ROWS = 6 * PIECE
SEND_ONE = GRAD_ROWS + 32
SEND_TWO = PIECE + 80
SWAP_ROWS = GRAD_ROWS + PIECE


def call(kernel, outs, scratch=(), ins=None, limit=16):
    one = not isinstance(outs, list)
    more = {} if ins is None else {"in_specs": ins}
    return pl.pallas_call(
        kernel,
        **more,
        out_shape=outs,
        out_specs=VM if one else [VM] * len(outs),
        scratch_shapes=list(scratch),
        compiler_params=pltpu.CompilerParams(vmem_limit_bytes=limit << 20),
    )


def tile_rows(piece, wide, groups):
    tiles = []
    for g in range(groups):
        block = piece(wide, g)
        tiles += [block[:, 160 * k : 160 * k + 160] for k in range(4)]
    return tiles


def read_block(ref, g):
    return ref[:, 640 * g : 640 * g + 640].astype(F32)


def every(offset, across=False):
    shape, short, long = ((256, 32), 1, 0) if across else ((32, 256), 0, 1)
    hit = lax.broadcasted_iota(jnp.int32, shape, long) == 8 * lax.broadcasted_iota(
        jnp.int32, shape, short
    ) + offset
    return hit.astype(F32).astype(BF16)


def pack(rows):
    tail = rows[:, 128:160]
    side = jnp.concatenate([tail[8 * b : 8 * b + 8] for b in range(4)], axis=1)
    return jnp.concatenate([rows[:, 0:128], side], axis=0)


def unpack(piece):
    side = piece[32:40]
    tail = jnp.concatenate([side[:, 32 * b : 32 * b + 32] for b in range(4)], axis=0)
    return jnp.concatenate([piece[0:32], tail], axis=1)


def prepare_kernel(
    image_hbm, cotan_hbm, weight_hbm,
    even_ref, odd_ref, cotan_ref, rows_ref, edge_ref, trade_ref,
    image_ref, own_ref, weight_ref, done,
):
    reads = [
        pltpu.make_async_copy(image_hbm, image_ref, done.at[0]),
        pltpu.make_async_copy(cotan_hbm, cotan_ref, done.at[1]),
        pltpu.make_async_copy(weight_hbm, own_ref, done.at[2]),
    ]
    for read in reads:
        read.start()
    for read in reads:
        read.wait()
    tiles = tile_rows(read_block, image_ref, 16)
    even = jnp.concatenate(tiles[0::2], axis=0).astype(BF16)
    odd = jnp.concatenate(tiles[1::2], axis=0).astype(BF16)
    even_ref[...] = even
    odd_ref[...] = odd
    flat = cotan_ref[...].astype(F32)
    edges = [
        jnp.dot(every(7), even, preferred_element_type=F32),
        jnp.dot(every(7), odd, preferred_element_type=F32),
        jnp.concatenate([flat[0:1, C * j : C * j + C] for j in range(32)], axis=0),
    ]
    for k in range(3):
        edge_ref[k] = pack(edges[k]).astype(BF16)
    first = lax.axis_index("core") == 0
    trade_ref[0] = jnp.where(first, edge_ref[2].astype(F32), edge_ref[0].astype(F32)).astype(BF16)
    trade_ref[1] = edge_ref[1]
    weight_ref[0:60] = own_ref[...]
    weight_ref[60:64] = jnp.zeros((4, C), F32)
    quarter = 2 * lax.axis_index("core") + lax.axis_index("zhi")
    mine = weight_ref[0:16]
    for q in range(1, 4):
        mine = jnp.where(quarter == q, weight_ref[15 * q : 15 * q + 16], mine)
    tail = mine[:, 128:160]
    lane = lax.broadcasted_iota(jnp.int32, (16, 128), 1) // 32
    tail = jnp.where(lane == lax.axis_index("x"), jnp.concatenate([tail] * 4, axis=1), 0.0)
    rows_ref[...] = jnp.concatenate([mine[:, 0:128], tail], axis=0).astype(BF16)


def grad_kernel(
    even_ref, odd_ref, cotan_ref, edge_ref,
    keep_ref, give_ref, taps_ref,
    five_ref, spread_ref, sums_ref,
):
    even = even_ref[...]
    odd = odd_ref[...]
    five_ref[...] = jnp.zeros_like(five_ref)
    five_ref[0:4] = cotan_ref[...].astype(F32)
    out_row = lax.broadcasted_iota(jnp.int32, (24, 8), 0)
    in_row = lax.broadcasted_iota(jnp.int32, (24, 8), 1)
    pick = (2 * in_row + out_row // 8 - 1 == out_row % 8).astype(F32).astype(BF16)
    spread_ref[...] = jnp.dot(pick, five_ref[...].astype(BF16), preferred_element_type=F32)
    taps = []
    for r in range(3):
        cols = tile_rows(lambda ref, g: ref[8 * r : 8 * r + 8, 640 * g : 640 * g + 640], spread_ref, 8)
        block = jnp.concatenate(cols, axis=0).astype(BF16)
        taps_ref[r] = block
        taps.append(block)
    zeros = jnp.zeros((8, C), BF16)

    def put(r, s, left, right):
        row = (3 * r + s) * C
        sums_ref[row : row + C] = lax.dot_general(
            left, right, (((0,), (0,)), ((), ())), preferred_element_type=F32
        )

    for r in range(3):
        put(r, 1, even, taps[r])
        put(r, 2, odd, taps[r])
        put(r, 0, odd[0:248], taps[r][8:256])
    sums_ref[1440:1448] = zeros.astype(F32)
    first = lax.axis_index("core") == 0
    for x in range(4):
        for low in range(6):
            start = 60 * (6 * x + low)
            halves = [pack(sums_ref[start + 30 * c : start + 30 * c + 32]) for c in range(2)]
            at = slice(PIECE * low, PIECE * low + PIECE)
            keep_ref[x, at] = jnp.where(first, halves[0], halves[1]).astype(BF16)
            give_ref[x, at] = jnp.where(first, halves[1], halves[0]).astype(BF16)
    for k in range(3):
        give_ref[k, GRAD_ROWS:SWAP_ROWS] = edge_ref[k]
    give_ref[3, GRAD_ROWS:SWAP_ROWS] = edge_ref[2]


def core_sum_kernel(
    keep_ref, got_ref, rows_ref, edge_ref, trade_ref,
    send_ref, below_ref, above_ref,
    edge_sum_ref,
):
    first = lax.axis_index("core") == 0
    mine = [unpack(edge_ref[k].astype(F32)) for k in range(3)]
    partner = [unpack(got_ref[k, GRAD_ROWS:SWAP_ROWS].astype(F32)) for k in range(3)]
    far = [unpack(trade_ref[k].astype(F32)) for k in range(2)]

    def choose(zero, one):
        return jnp.where(first, zero, one)

    inner_cotan, outer_cotan = choose(partner[2], mine[2]), choose(mine[2], far[0])
    zero = jnp.zeros((1, C), F32)
    rights = [
        jnp.concatenate([inner_cotan[1:32], zero, outer_cotan[1:32], zero], axis=0).astype(BF16),
        jnp.concatenate([inner_cotan, outer_cotan], axis=0).astype(BF16),
    ]
    even, odd = [
        jnp.concatenate(
            [choose(mine[k], partner[k]), choose(far[k], mine[k])], axis=0
        ).astype(BF16)
        for k in range(2)
    ]
    below_ref[...] = choose(partner[2], far[0]).astype(BF16)
    for k in range(2):
        above_ref[k] = choose(far[k], partner[k]).astype(BF16)
    edge_sum_ref[480:512] = jnp.zeros((32, C), F32)
    for s, left in ((0, odd), (1, even), (2, odd)):
        edge_sum_ref[C * s : C * s + C] = lax.dot_general(
            left, rights[min(s, 1)], (((0,), (0,)), ((), ())), preferred_element_type=F32
        )
    for x in range(4):
        total = keep_ref[x].astype(F32) + got_ref[x, 0:GRAD_ROWS].astype(F32)
        parts = []
        for low in range(6):
            part = total[PIECE * low : PIECE * low + PIECE]
            start = 60 * (6 * x + low)
            if start < 480:
                halves = [edge_sum_ref[start + 30 * c : start + 30 * c + 32] for c in range(2)]
                part = part + pack(choose(*halves))
            parts.append(part)
        send_ref[x, 0:GRAD_ROWS] = jnp.concatenate(parts, axis=0).astype(BF16)
        send_ref[x, GRAD_ROWS:SEND_ONE] = rows_ref[...]


def first_sum_kernel(got_ref, send_ref):
    total = got_ref[0, 0:GRAD_ROWS].astype(F32)
    tail = got_ref[0, GRAD_ROWS + 16 : SEND_ONE].astype(F32)
    for x in range(1, 4):
        total = total + got_ref[x, 0:GRAD_ROWS].astype(F32)
        tail = tail + got_ref[x, GRAD_ROWS + 16 : SEND_ONE].astype(F32)
    total = total.astype(BF16)
    tail = tail.astype(BF16)
    heads = [got_ref[x, GRAD_ROWS : GRAD_ROWS + 16] for x in range(4)]
    for low in range(6):
        for high in range(2):
            n = 2 * low + high
            send_ref[n, 0:PIECE] = total[PIECE * low : PIECE * low + PIECE]
            for x in range(4):
                send_ref[n, PIECE + 16 * x : PIECE + 16 * x + 16] = heads[x]
            send_ref[n, PIECE + 64 : SEND_TWO] = tail


def second_sum_kernel(got_ref, send_ref):
    total = got_ref[0, 0:PIECE].astype(F32)
    for n in range(1, 12):
        total = total + got_ref[n, 0:PIECE].astype(F32)
    total = total.astype(BF16)
    for n in range(16):
        send_ref[n] = total


def conv_kernel(
    even_ref, odd_ref, taps_ref, below_ref, above_ref, own_ref, other_ref,
    out_ref, grad_ref,
    kernel_ref, shift_ref, roll_ref,
):
    core = lax.axis_index("core")
    for x in range(4):
        for low in range(6):
            for c in range(2):
                for high in range(2):
                    n = 2 * low + high
                    own = own_ref[n, PIECE:SEND_TWO].astype(F32)
                    other = other_ref[n, PIECE:SEND_TWO].astype(F32)
                    block = jnp.where(core == c, own, other)
                    start = 60 * (6 * x + low) + 15 * (2 * c + high)
                    kernel_ref[start : start + 16] = jnp.concatenate(
                        [block[16 * x : 16 * x + 16], block[64:80, 32 * x : 32 * x + 32]], axis=1
                    )

    def tap(r, s):
        row = (3 * r + s) * C
        return kernel_ref[row : row + C].astype(BF16)

    def dot(left, right):
        return jnp.dot(left, right, preferred_element_type=F32)

    def dot_t(left, right):
        return lax.dot_general(left, right, (((1,), (1,)), ((), ())), preferred_element_type=F32)

    zeros = jnp.zeros((8, C), BF16)
    even = even_ref[...]
    odd = odd_ref[...]
    odd_before = jnp.concatenate([zeros, odd[0:248]], axis=0)
    start_row = lax.broadcasted_iota(jnp.int32, (256, C), 0) % 8 == 0

    def down(columns, above):
        shift_ref[8:264] = columns.astype(F32)
        top = jnp.dot(every(0, True), above, preferred_element_type=F32)
        return jnp.where(start_row, top, shift_ref[7:263]).astype(BF16)

    shift_ref[0:8] = jnp.zeros((8, C), F32)
    even_down = down(even, above_ref[0])
    odd_down = down(odd, above_ref[1])
    odd_down_before = jnp.concatenate([zeros, odd_down[0:248]], axis=0)
    roll_ref[0:256] = dot(even, tap(2, 1)) + dot(odd, tap(2, 2)) + dot(odd_before, tap(2, 0))
    roll_ref[256:264] = jnp.zeros((8, C), F32)
    total = dot(even_down, tap(0, 1)) + dot(odd_down, tap(0, 2)) + dot(odd_down_before, tap(0, 0))
    total = total + dot(even, tap(1, 1)) + dot(odd, tap(1, 2)) + dot(odd_before, tap(1, 0))
    total = total + roll_ref[1:257]
    for g in range(8):
        wide = jnp.concatenate(
            [total[32 * g + 8 * k : 32 * g + 8 * k + 8] for k in range(4)], axis=1
        )
        rows = jnp.concatenate([wide[2 * i : 2 * i + 1] for i in range(4)], axis=0)
        out_ref[:, 640 * g : 640 * g + 640] = rows.astype(BF16)
    taps = [taps_ref[r] for r in range(3)]
    last = jnp.dot(every(7, True), below_ref[...], preferred_element_type=F32)
    taps[0] = (taps[0].astype(F32) + last).astype(BF16)
    after = [jnp.concatenate([t[8:256], zeros], axis=0) for t in taps]
    grad_even = dot_t(taps[0], tap(0, 1)) + dot_t(taps[1], tap(1, 1)) + dot_t(taps[2], tap(2, 1))
    grad_odd = dot_t(taps[0], tap(0, 2)) + dot_t(taps[1], tap(1, 2)) + dot_t(taps[2], tap(2, 2))
    for r in range(3):
        grad_odd = grad_odd + dot_t(after[r], tap(r, 0))
    for g in range(16):
        parts = []
        for k in range(2):
            row = 16 * g + 8 * k
            parts += [grad_even[row : row + 8], grad_odd[row : row + 8]]
        grad_ref[:, 640 * g : 640 * g + 640] = jnp.concatenate(parts, axis=1).astype(BF16)


def adam_kernel(got_ref, weight_ref, one_ref, two_ref, new_weight_ref, new_one_ref, new_two_ref, sums_ref):
    for core in range(2):
        total = got_ref[core].astype(F32)
        for y in range(1, 8):
            total = total + got_ref[2 * y + core].astype(F32)
        sums_ref[30 * core : 30 * core + 32] = unpack(total)
    gradient = sums_ref[0:60] / float(COUNT)
    weight = weight_ref[...]
    new_one = beta_one * one_ref[...] + (1.0 - beta_one) * gradient
    new_two = beta_two * two_ref[...] + (1.0 - beta_two) * gradient * gradient
    first_hat = new_one / (1.0 - beta_one**adam_step)
    second_hat = new_two / (1.0 - beta_two**adam_step)
    new_weight_ref[...] = weight - learn_rate * (
        first_hat / (jnp.sqrt(second_hat) + epsilon) + decay_rate * weight
    )
    new_one_ref[...] = new_one
    new_two_ref[...] = new_two


def body(image, cotangent, weight, moment_one, moment_two):
    shape = jax.ShapeDtypeStruct
    image = image.reshape(8, 64 * C)
    cotangent = cotangent.reshape(4, 32 * C)
    even, odd, strip, rows, edge, trade = call(
        prepare_kernel,
        [
            shape((256, C), BF16),
            shape((256, C), BF16),
            shape((4, 32 * C), BF16),
            shape((32, 128), BF16),
            shape((3, PIECE, 128), BF16),
            shape((2, PIECE, 128), BF16),
        ],
        [
            pltpu.VMEM((8, 64 * C), BF16),
            pltpu.VMEM((60, C), F32),
            pltpu.VMEM((64, C), F32),
            pltpu.SemaphoreType.DMA((3,)),
        ],
        [pl.BlockSpec(memory_space=pltpu.HBM)] * 3,
    )(*[pltpu.with_memory_space_constraint(a, pltpu.HBM) for a in (image, cotangent, weight)])
    route = [(i, i - 1 if i % 2 == 0 else i + 1) for i in range(1, 31)]
    traded = lax.ppermute(trade, ("zhi", "y", "core"), route)
    keep, give, taps = call(
        grad_kernel,
        [
            shape((4, GRAD_ROWS, 128), BF16),
            shape((4, SWAP_ROWS, 128), BF16),
            shape((3, 256, C), BF16),
        ],
        [
            pltpu.VMEM((8, 32 * C), F32),
            pltpu.VMEM((24, 32 * C), F32),
            pltpu.VMEM((1448, C), F32),
        ],
    )(even, odd, strip, edge)
    given = lax.ppermute(give, "core", [(0, 1), (1, 0)])
    send_one, below, above = call(
        core_sum_kernel,
        [shape((4, SEND_ONE, 128), BF16), shape((32, C), BF16), shape((2, 32, C), BF16)],
        [pltpu.VMEM((512, C), F32)],
    )(keep, given, rows, edge, traded)
    got_one = lax.all_to_all(send_one, "x", 0, 0, tiled=True)
    send_two = call(first_sum_kernel, shape((12, SEND_TWO, 128), BF16))(got_one)
    got_two = lax.all_to_all(send_two, ("zlo", "zhi"), 0, 0, tiled=True)
    other = lax.ppermute(got_two, "core", [(0, 1), (1, 0)])
    send_three = call(second_sum_kernel, shape((16, PIECE, 128), BF16))(got_two)
    got_three = lax.all_to_all(send_three, ("y", "core"), 0, 0, tiled=True)
    output, grad_image = call(
        conv_kernel,
        [shape((4, 32 * C), BF16), shape((8, 64 * C), BF16)],
        [
            pltpu.VMEM((1448, C), F32),
            pltpu.VMEM((264, C), F32),
            pltpu.VMEM((264, C), F32),
        ],
    )(even, odd, taps, below, above, got_two, other)
    new_weight, new_one, new_two = call(
        adam_kernel, [shape((60, C), F32)] * 3, [pltpu.VMEM((64, C), F32)]
    )(got_three, weight, moment_one, moment_two)
    return (output[None], grad_image[None], new_weight, new_one, new_two)


def solution(mesh):
    fine = Mesh(mesh.devices.reshape(4, 6, 2, 8, 2), ("x", "zlo", "zhi", "y", "core"))
    dp, space = ("x", "zlo"), ("zhi", "y", "core")
    specs = (P(dp, space, None), P(dp, space, None), P(dp, None), P(dp, None), P(dp, None))

    return jax.shard_map(body, mesh=fine, in_specs=specs, out_specs=specs, check_vma=False)
```

```python
import jax
import jax.numpy as jnp
from jax import lax
from jax.experimental import pallas as pl
from jax.experimental.pallas import tpu as pltpu
from jax.sharding import Mesh
from jax.sharding import PartitionSpec as P


beta_one = 0.9
beta_two = 0.999
learn_rate = 0.01
decay_rate = 0.01
epsilon = 1e-08
adam_step = 10

C = 160
COUNT = 98304
F32 = jnp.float32
BF16 = jnp.bfloat16
VM = pl.BlockSpec(memory_space=pltpu.VMEM)

PIECE = 40
GRAD_ROWS = 6 * PIECE
SEND_ONE = GRAD_ROWS + 32
SEND_TWO = PIECE + 80
SWAP_ROWS = GRAD_ROWS + PIECE


def call(kernel, outs, scratch=(), ins=None, limit=16):
    one = not isinstance(outs, list)
    more = {} if ins is None else {"in_specs": ins}
    return pl.pallas_call(
        kernel,
        **more,
        out_shape=outs,
        out_specs=VM if one else [VM] * len(outs),
        scratch_shapes=list(scratch),
        compiler_params=pltpu.CompilerParams(vmem_limit_bytes=limit << 20),
    )


def tile_rows(piece, wide, groups):
    tiles = []
    for g in range(groups):
        block = piece(wide, g)
        tiles += [block[:, 160 * k : 160 * k + 160] for k in range(4)]
    return tiles


def read_block(ref, g):
    return ref[:, 640 * g : 640 * g + 640].astype(F32)


def every(offset, across=False):
    shape, short, long = ((256, 32), 1, 0) if across else ((32, 256), 0, 1)
    hit = lax.broadcasted_iota(jnp.int32, shape, long) == 8 * lax.broadcasted_iota(
        jnp.int32, shape, short
    ) + offset
    return hit.astype(F32).astype(BF16)


def pack(rows):
    tail = rows[:, 128:160]
    side = jnp.concatenate([tail[8 * b : 8 * b + 8] for b in range(4)], axis=1)
    return jnp.concatenate([rows[:, 0:128], side], axis=0)


def unpack(piece):
    side = piece[32:40]
    tail = jnp.concatenate([side[:, 32 * b : 32 * b + 32] for b in range(4)], axis=0)
    return jnp.concatenate([piece[0:32], tail], axis=1)


def prepare_kernel(
    image_hbm, cotan_hbm, weight_hbm,
    even_ref, odd_ref, cotan_ref, rows_ref, edge_ref, trade_ref,
    image_ref, own_ref, weight_ref, done,
):
    reads = [
        pltpu.make_async_copy(image_hbm, image_ref, done.at[0]),
        pltpu.make_async_copy(cotan_hbm, cotan_ref, done.at[1]),
        pltpu.make_async_copy(weight_hbm, own_ref, done.at[2]),
    ]
    for read in reads:
        read.start()
    for read in reads:
        read.wait()
    tiles = tile_rows(read_block, image_ref, 16)
    even = jnp.concatenate(tiles[0::2], axis=0).astype(BF16)
    odd = jnp.concatenate(tiles[1::2], axis=0).astype(BF16)
    even_ref[...] = even
    odd_ref[...] = odd
    flat = cotan_ref[...].astype(F32)
    edges = [
        jnp.dot(every(7), even, preferred_element_type=F32),
        jnp.dot(every(7), odd, preferred_element_type=F32),
        jnp.concatenate([flat[0:1, C * j : C * j + C] for j in range(32)], axis=0),
    ]
    for k in range(3):
        edge_ref[k] = pack(edges[k]).astype(BF16)
    first = lax.axis_index("core") == 0
    trade_ref[0] = jnp.where(first, edge_ref[2].astype(F32), edge_ref[0].astype(F32)).astype(BF16)
    trade_ref[1] = edge_ref[1]
    weight_ref[0:60] = own_ref[...]
    weight_ref[60:64] = jnp.zeros((4, C), F32)
    quarter = 2 * lax.axis_index("core") + lax.axis_index("zhi")
    mine = weight_ref[0:16]
    for q in range(1, 4):
        mine = jnp.where(quarter == q, weight_ref[15 * q : 15 * q + 16], mine)
    tail = mine[:, 128:160]
    lane = lax.broadcasted_iota(jnp.int32, (16, 128), 1) // 32
    tail = jnp.where(lane == lax.axis_index("x"), jnp.concatenate([tail] * 4, axis=1), 0.0)
    rows_ref[...] = jnp.concatenate([mine[:, 0:128], tail], axis=0).astype(BF16)


def grad_kernel(
    even_ref, odd_ref, cotan_ref, edge_ref,
    keep_ref, give_ref, taps_ref,
    five_ref, spread_ref, sums_ref,
):
    even = even_ref[...]
    odd = odd_ref[...]
    five_ref[...] = jnp.zeros_like(five_ref)
    five_ref[0:4] = cotan_ref[...].astype(F32)
    out_row = lax.broadcasted_iota(jnp.int32, (24, 8), 0)
    in_row = lax.broadcasted_iota(jnp.int32, (24, 8), 1)
    pick = (2 * in_row + out_row // 8 - 1 == out_row % 8).astype(F32).astype(BF16)
    spread_ref[...] = jnp.dot(pick, five_ref[...].astype(BF16), preferred_element_type=F32)
    taps = []
    for r in range(3):
        cols = tile_rows(lambda ref, g: ref[8 * r : 8 * r + 8, 640 * g : 640 * g + 640], spread_ref, 8)
        block = jnp.concatenate(cols, axis=0).astype(BF16)
        taps_ref[r] = block
        taps.append(block)
    zeros = jnp.zeros((8, C), BF16)

    def put(r, s, left, right):
        row = (3 * r + s) * C
        sums_ref[row : row + C] = lax.dot_general(
            left, right, (((0,), (0,)), ((), ())), preferred_element_type=F32
        )

    for r in range(3):
        put(r, 1, even, taps[r])
        put(r, 2, odd, taps[r])
        put(r, 0, odd[0:248], taps[r][8:256])
    sums_ref[1440:1448] = zeros.astype(F32)
    first = lax.axis_index("core") == 0
    for x in range(4):
        for low in range(6):
            start = 60 * (6 * x + low)
            halves = [pack(sums_ref[start + 30 * c : start + 30 * c + 32]) for c in range(2)]
            at = slice(PIECE * low, PIECE * low + PIECE)
            keep_ref[x, at] = jnp.where(first, halves[0], halves[1]).astype(BF16)
            give_ref[x, at] = jnp.where(first, halves[1], halves[0]).astype(BF16)
    for k in range(3):
        give_ref[k, GRAD_ROWS:SWAP_ROWS] = edge_ref[k]
    give_ref[3, GRAD_ROWS:SWAP_ROWS] = edge_ref[2]


def core_sum_kernel(
    keep_ref, got_ref, rows_ref, edge_ref, trade_ref,
    send_ref, below_ref, above_ref,
    edge_sum_ref,
):
    first = lax.axis_index("core") == 0
    mine = [unpack(edge_ref[k].astype(F32)) for k in range(3)]
    partner = [unpack(got_ref[k, GRAD_ROWS:SWAP_ROWS].astype(F32)) for k in range(3)]
    far = [unpack(trade_ref[k].astype(F32)) for k in range(2)]

    def choose(zero, one):
        return jnp.where(first, zero, one)

    inner_cotan, outer_cotan = choose(partner[2], mine[2]), choose(mine[2], far[0])
    zero = jnp.zeros((1, C), F32)
    rights = [
        jnp.concatenate([inner_cotan[1:32], zero, outer_cotan[1:32], zero], axis=0).astype(BF16),
        jnp.concatenate([inner_cotan, outer_cotan], axis=0).astype(BF16),
    ]
    even, odd = [
        jnp.concatenate(
            [choose(mine[k], partner[k]), choose(far[k], mine[k])], axis=0
        ).astype(BF16)
        for k in range(2)
    ]
    below_ref[...] = choose(partner[2], far[0]).astype(BF16)
    for k in range(2):
        above_ref[k] = choose(far[k], partner[k]).astype(BF16)
    edge_sum_ref[480:512] = jnp.zeros((32, C), F32)
    for s, left in ((0, odd), (1, even), (2, odd)):
        edge_sum_ref[C * s : C * s + C] = lax.dot_general(
            left, rights[min(s, 1)], (((0,), (0,)), ((), ())), preferred_element_type=F32
        )
    for x in range(4):
        total = keep_ref[x].astype(F32) + got_ref[x, 0:GRAD_ROWS].astype(F32)
        parts = []
        for low in range(6):
            part = total[PIECE * low : PIECE * low + PIECE]
            start = 60 * (6 * x + low)
            if start < 480:
                halves = [edge_sum_ref[start + 30 * c : start + 30 * c + 32] for c in range(2)]
                part = part + pack(choose(*halves))
            parts.append(part)
        send_ref[x, 0:GRAD_ROWS] = jnp.concatenate(parts, axis=0).astype(BF16)
        send_ref[x, GRAD_ROWS:SEND_ONE] = rows_ref[...]


def first_sum_kernel(got_ref, send_ref):
    total = got_ref[0, 0:GRAD_ROWS].astype(F32)
    tail = got_ref[0, GRAD_ROWS + 16 : SEND_ONE].astype(F32)
    for x in range(1, 4):
        total = total + got_ref[x, 0:GRAD_ROWS].astype(F32)
        tail = tail + got_ref[x, GRAD_ROWS + 16 : SEND_ONE].astype(F32)
    total = total.astype(BF16)
    tail = tail.astype(BF16)
    heads = [got_ref[x, GRAD_ROWS : GRAD_ROWS + 16] for x in range(4)]
    for low in range(6):
        for high in range(2):
            n = 6 * high + low
            send_ref[n, 0:PIECE] = total[PIECE * low : PIECE * low + PIECE]
            for x in range(4):
                send_ref[n, PIECE + 16 * x : PIECE + 16 * x + 16] = heads[x]
            send_ref[n, PIECE + 64 : SEND_TWO] = tail


def second_sum_kernel(got_ref, send_ref):
    total = got_ref[0, 0:PIECE].astype(F32)
    for n in range(1, 12):
        total = total + got_ref[n, 0:PIECE].astype(F32)
    total = total.astype(BF16)
    for n in range(16):
        send_ref[n] = total


def conv_kernel(
    even_ref, odd_ref, taps_ref, below_ref, above_ref, own_ref, other_ref,
    out_ref, grad_ref,
    kernel_ref, shift_ref, roll_ref,
):
    core = lax.axis_index("core")
    for x in range(4):
        for low in range(6):
            for c in range(2):
                for high in range(2):
                    n = 6 * high + low
                    own = own_ref[n, PIECE:SEND_TWO].astype(F32)
                    other = other_ref[n, PIECE:SEND_TWO].astype(F32)
                    block = jnp.where(core == c, own, other)
                    start = 60 * (6 * x + low) + 15 * (2 * c + high)
                    kernel_ref[start : start + 16] = jnp.concatenate(
                        [block[16 * x : 16 * x + 16], block[64:80, 32 * x : 32 * x + 32]], axis=1
                    )

    def tap(r, s):
        row = (3 * r + s) * C
        return kernel_ref[row : row + C].astype(BF16)

    def dot(left, right):
        return jnp.dot(left, right, preferred_element_type=F32)

    def dot_t(left, right):
        return lax.dot_general(left, right, (((1,), (1,)), ((), ())), preferred_element_type=F32)

    zeros = jnp.zeros((8, C), BF16)
    even = even_ref[...]
    odd = odd_ref[...]
    odd_before = jnp.concatenate([zeros, odd[0:248]], axis=0)
    start_row = lax.broadcasted_iota(jnp.int32, (256, C), 0) % 8 == 0

    def down(columns, above):
        shift_ref[8:264] = columns.astype(F32)
        top = jnp.dot(every(0, True), above, preferred_element_type=F32)
        return jnp.where(start_row, top, shift_ref[7:263]).astype(BF16)

    shift_ref[0:8] = jnp.zeros((8, C), F32)
    even_down = down(even, above_ref[0])
    odd_down = down(odd, above_ref[1])
    odd_down_before = jnp.concatenate([zeros, odd_down[0:248]], axis=0)
    roll_ref[0:256] = dot(even, tap(2, 1)) + dot(odd, tap(2, 2)) + dot(odd_before, tap(2, 0))
    roll_ref[256:264] = jnp.zeros((8, C), F32)
    total = dot(even_down, tap(0, 1)) + dot(odd_down, tap(0, 2)) + dot(odd_down_before, tap(0, 0))
    total = total + dot(even, tap(1, 1)) + dot(odd, tap(1, 2)) + dot(odd_before, tap(1, 0))
    total = total + roll_ref[1:257]
    for g in range(8):
        wide = jnp.concatenate(
            [total[32 * g + 8 * k : 32 * g + 8 * k + 8] for k in range(4)], axis=1
        )
        rows = jnp.concatenate([wide[2 * i : 2 * i + 1] for i in range(4)], axis=0)
        out_ref[:, 640 * g : 640 * g + 640] = rows.astype(BF16)
    taps = [taps_ref[r] for r in range(3)]
    last = jnp.dot(every(7, True), below_ref[...], preferred_element_type=F32)
    taps[0] = (taps[0].astype(F32) + last).astype(BF16)
    after = [jnp.concatenate([t[8:256], zeros], axis=0) for t in taps]
    grad_even = dot_t(taps[0], tap(0, 1)) + dot_t(taps[1], tap(1, 1)) + dot_t(taps[2], tap(2, 1))
    grad_odd = dot_t(taps[0], tap(0, 2)) + dot_t(taps[1], tap(1, 2)) + dot_t(taps[2], tap(2, 2))
    for r in range(3):
        grad_odd = grad_odd + dot_t(after[r], tap(r, 0))
    for g in range(16):
        parts = []
        for k in range(2):
            row = 16 * g + 8 * k
            parts += [grad_even[row : row + 8], grad_odd[row : row + 8]]
        grad_ref[:, 640 * g : 640 * g + 640] = jnp.concatenate(parts, axis=1).astype(BF16)


def adam_kernel(got_ref, weight_ref, one_ref, two_ref, new_weight_ref, new_one_ref, new_two_ref, sums_ref):
    for core in range(2):
        total = got_ref[core].astype(F32)
        for y in range(1, 8):
            total = total + got_ref[2 * y + core].astype(F32)
        sums_ref[30 * core : 30 * core + 32] = unpack(total)
    gradient = sums_ref[0:60] / float(COUNT)
    weight = weight_ref[...]
    new_one = beta_one * one_ref[...] + (1.0 - beta_one) * gradient
    new_two = beta_two * two_ref[...] + (1.0 - beta_two) * gradient * gradient
    first_hat = new_one / (1.0 - beta_one**adam_step)
    second_hat = new_two / (1.0 - beta_two**adam_step)
    new_weight_ref[...] = weight - learn_rate * (
        first_hat / (jnp.sqrt(second_hat) + epsilon) + decay_rate * weight
    )
    new_one_ref[...] = new_one
    new_two_ref[...] = new_two


def body(image, cotangent, weight, moment_one, moment_two):
    shape = jax.ShapeDtypeStruct
    image = image.reshape(8, 64 * C)
    cotangent = cotangent.reshape(4, 32 * C)
    even, odd, strip, rows, edge, trade = call(
        prepare_kernel,
        [
            shape((256, C), BF16),
            shape((256, C), BF16),
            shape((4, 32 * C), BF16),
            shape((32, 128), BF16),
            shape((3, PIECE, 128), BF16),
            shape((2, PIECE, 128), BF16),
        ],
        [
            pltpu.VMEM((8, 64 * C), BF16),
            pltpu.VMEM((60, C), F32),
            pltpu.VMEM((64, C), F32),
            pltpu.SemaphoreType.DMA((3,)),
        ],
        [pl.BlockSpec(memory_space=pltpu.HBM)] * 3,
    )(*[pltpu.with_memory_space_constraint(a, pltpu.HBM) for a in (image, cotangent, weight)])
    route = [(i, i - 1 if i % 2 == 0 else i + 1) for i in range(1, 31)]
    traded = lax.ppermute(trade, ("zhi", "y", "core"), route)
    keep, give, taps = call(
        grad_kernel,
        [
            shape((4, GRAD_ROWS, 128), BF16),
            shape((4, SWAP_ROWS, 128), BF16),
            shape((3, 256, C), BF16),
        ],
        [
            pltpu.VMEM((8, 32 * C), F32),
            pltpu.VMEM((24, 32 * C), F32),
            pltpu.VMEM((1448, C), F32),
        ],
    )(even, odd, strip, edge)
    given = lax.ppermute(give, "core", [(0, 1), (1, 0)])
    send_one, below, above = call(
        core_sum_kernel,
        [shape((4, SEND_ONE, 128), BF16), shape((32, C), BF16), shape((2, 32, C), BF16)],
        [pltpu.VMEM((512, C), F32)],
    )(keep, given, rows, edge, traded)
    got_one = lax.all_to_all(send_one, "x", 0, 0, tiled=True)
    send_two = call(first_sum_kernel, shape((12, SEND_TWO, 128), BF16))(got_one)
    got_two = lax.all_to_all(send_two, ("zhi", "zlo"), 0, 0, tiled=True)
    other = lax.ppermute(got_two, "core", [(0, 1), (1, 0)])
    send_three = call(second_sum_kernel, shape((16, PIECE, 128), BF16))(got_two)
    got_three = lax.all_to_all(send_three, ("y", "core"), 0, 0, tiled=True)
    output, grad_image = call(
        conv_kernel,
        [shape((4, 32 * C), BF16), shape((8, 64 * C), BF16)],
        [
            pltpu.VMEM((1448, C), F32),
            pltpu.VMEM((264, C), F32),
            pltpu.VMEM((264, C), F32),
        ],
    )(even, odd, taps, below, above, got_two, other)
    new_weight, new_one, new_two = call(
        adam_kernel, [shape((60, C), F32)] * 3, [pltpu.VMEM((64, C), F32)]
    )(got_three, weight, moment_one, moment_two)
    return (output[None], grad_image[None], new_weight, new_one, new_two)


def solution(mesh):
    fine = Mesh(mesh.devices.reshape(4, 6, 2, 8, 2), ("x", "zlo", "zhi", "y", "core"))
    dp, space = ("x", "zlo"), ("zhi", "y", "core")
    specs = (P(dp, space, None), P(dp, space, None), P(dp, None), P(dp, None), P(dp, None))

    return jax.shard_map(body, mesh=fine, in_specs=specs, out_specs=specs, check_vma=False)
```

```python
import jax
import jax.numpy as jnp
from jax import lax
from jax.experimental import pallas as pl
from jax.experimental.pallas import tpu as pltpu
from jax.sharding import Mesh
from jax.sharding import PartitionSpec as P


beta_one = 0.9
beta_two = 0.999
learn_rate = 0.01
decay_rate = 0.01
epsilon = 1e-08
adam_step = 10

C = 160
COUNT = 98304
F32 = jnp.float32
BF16 = jnp.bfloat16
VM = pl.BlockSpec(memory_space=pltpu.VMEM)

PIECE = 40
GRAD_ROWS = 6 * PIECE
SEND_ONE = GRAD_ROWS + 32
SEND_TWO = PIECE + 80
SWAP_ROWS = GRAD_ROWS + PIECE


def call(kernel, outs, scratch=(), ins=None, limit=16):
    one = not isinstance(outs, list)
    more = {} if ins is None else {"in_specs": ins}
    return pl.pallas_call(
        kernel,
        **more,
        out_shape=outs,
        out_specs=VM if one else [VM] * len(outs),
        scratch_shapes=list(scratch),
        compiler_params=pltpu.CompilerParams(vmem_limit_bytes=limit << 20),
    )


def tile_rows(piece, wide, groups):
    tiles = []
    for g in range(groups):
        block = piece(wide, g)
        tiles += [block[:, 160 * k : 160 * k + 160] for k in range(4)]
    return tiles


def read_block(ref, g):
    return ref[:, 640 * g : 640 * g + 640].astype(F32)


def every(offset, across=False):
    shape, short, long = ((256, 32), 1, 0) if across else ((32, 256), 0, 1)
    hit = lax.broadcasted_iota(jnp.int32, shape, long) == 8 * lax.broadcasted_iota(
        jnp.int32, shape, short
    ) + offset
    return hit.astype(F32).astype(BF16)


def pack(rows):
    tail = rows[:, 128:160]
    side = jnp.concatenate([tail[8 * b : 8 * b + 8] for b in range(4)], axis=1)
    return jnp.concatenate([rows[:, 0:128], side], axis=0)


def unpack(piece):
    side = piece[32:40]
    tail = jnp.concatenate([side[:, 32 * b : 32 * b + 32] for b in range(4)], axis=0)
    return jnp.concatenate([piece[0:32], tail], axis=1)


def prepare_kernel(
    image_hbm, cotan_hbm, weight_hbm,
    even_ref, odd_ref, cotan_ref, rows_ref, edge_ref, trade_ref,
    image_ref, own_ref, weight_ref, done,
):
    reads = [
        pltpu.make_async_copy(image_hbm, image_ref, done.at[0]),
        pltpu.make_async_copy(cotan_hbm, cotan_ref, done.at[1]),
        pltpu.make_async_copy(weight_hbm, own_ref, done.at[2]),
    ]
    for read in reads:
        read.start()
    for read in reads:
        read.wait()
    tiles = tile_rows(read_block, image_ref, 16)
    even = jnp.concatenate(tiles[0::2], axis=0).astype(BF16)
    odd = jnp.concatenate(tiles[1::2], axis=0).astype(BF16)
    even_ref[...] = even
    odd_ref[...] = odd
    flat = cotan_ref[...].astype(F32)
    edges = [
        jnp.dot(every(7), even, preferred_element_type=F32),
        jnp.dot(every(7), odd, preferred_element_type=F32),
        jnp.concatenate([flat[0:1, C * j : C * j + C] for j in range(32)], axis=0),
    ]
    for k in range(3):
        edge_ref[k] = pack(edges[k]).astype(BF16)
    first = lax.axis_index("core") == 0
    trade_ref[0] = jnp.where(first, edge_ref[2].astype(F32), edge_ref[0].astype(F32)).astype(BF16)
    trade_ref[1] = edge_ref[1]
    weight_ref[0:60] = own_ref[...]
    weight_ref[60:64] = jnp.zeros((4, C), F32)
    quarter = 2 * lax.axis_index("core") + lax.axis_index("zhi")
    mine = weight_ref[0:16]
    for q in range(1, 4):
        mine = jnp.where(quarter == q, weight_ref[15 * q : 15 * q + 16], mine)
    tail = mine[:, 128:160]
    lane = lax.broadcasted_iota(jnp.int32, (16, 128), 1) // 32
    tail = jnp.where(lane == lax.axis_index("x"), jnp.concatenate([tail] * 4, axis=1), 0.0)
    rows_ref[...] = jnp.concatenate([mine[:, 0:128], tail], axis=0).astype(BF16)


def grad_kernel(
    even_ref, odd_ref, cotan_ref, edge_ref,
    keep_ref, give_ref, taps_ref,
    five_ref, spread_ref, sums_ref,
):
    even = even_ref[...]
    odd = odd_ref[...]
    five_ref[...] = jnp.zeros_like(five_ref)
    five_ref[0:4] = cotan_ref[...].astype(F32)
    out_row = lax.broadcasted_iota(jnp.int32, (24, 8), 0)
    in_row = lax.broadcasted_iota(jnp.int32, (24, 8), 1)
    pick = (2 * in_row + out_row // 8 - 1 == out_row % 8).astype(F32).astype(BF16)
    spread_ref[...] = jnp.dot(pick, five_ref[...].astype(BF16), preferred_element_type=F32)
    taps = []
    for r in range(3):
        cols = tile_rows(lambda ref, g: ref[8 * r : 8 * r + 8, 640 * g : 640 * g + 640], spread_ref, 8)
        block = jnp.concatenate(cols, axis=0).astype(BF16)
        taps_ref[r] = block
        taps.append(block)
    zeros = jnp.zeros((8, C), BF16)

    def put(r, s, left, right):
        row = (3 * r + s) * C
        sums_ref[row : row + C] = lax.dot_general(
            left, right, (((0,), (0,)), ((), ())), preferred_element_type=F32
        )

    for r in range(3):
        put(r, 1, even, taps[r])
        put(r, 2, odd, taps[r])
        put(r, 0, odd[0:248], taps[r][8:256])
    sums_ref[1440:1448] = zeros.astype(F32)
    first = lax.axis_index("core") == 0
    for x in range(4):
        for low in range(6):
            start = 60 * (6 * x + low)
            halves = [pack(sums_ref[start + 30 * c : start + 30 * c + 32]) for c in range(2)]
            at = slice(PIECE * low, PIECE * low + PIECE)
            keep_ref[x, at] = jnp.where(first, halves[0], halves[1]).astype(BF16)
            give_ref[x, at] = jnp.where(first, halves[1], halves[0]).astype(BF16)
    for k in range(3):
        give_ref[k, GRAD_ROWS:SWAP_ROWS] = edge_ref[k]
    give_ref[3, GRAD_ROWS:SWAP_ROWS] = edge_ref[2]


def core_sum_kernel(
    keep_ref, got_ref, rows_ref, edge_ref, trade_ref,
    send_ref, below_ref, above_ref,
    edge_sum_ref,
):
    first = lax.axis_index("core") == 0
    mine = [unpack(edge_ref[k].astype(F32)) for k in range(3)]
    partner = [unpack(got_ref[k, GRAD_ROWS:SWAP_ROWS].astype(F32)) for k in range(3)]
    far = [unpack(trade_ref[k].astype(F32)) for k in range(2)]

    def choose(zero, one):
        return jnp.where(first, zero, one)

    inner_cotan, outer_cotan = choose(partner[2], mine[2]), choose(mine[2], far[0])
    zero = jnp.zeros((1, C), F32)
    rights = [
        jnp.concatenate([inner_cotan[1:32], zero, outer_cotan[1:32], zero], axis=0).astype(BF16),
        jnp.concatenate([inner_cotan, outer_cotan], axis=0).astype(BF16),
    ]
    even, odd = [
        jnp.concatenate(
            [choose(mine[k], partner[k]), choose(far[k], mine[k])], axis=0
        ).astype(BF16)
        for k in range(2)
    ]
    below_ref[...] = choose(partner[2], far[0]).astype(BF16)
    for k in range(2):
        above_ref[k] = choose(far[k], partner[k]).astype(BF16)
    edge_sum_ref[480:512] = jnp.zeros((32, C), F32)
    for s, left in ((0, odd), (1, even), (2, odd)):
        edge_sum_ref[C * s : C * s + C] = lax.dot_general(
            left, rights[min(s, 1)], (((0,), (0,)), ((), ())), preferred_element_type=F32
        )
    for x in range(4):
        total = keep_ref[x].astype(F32) + got_ref[x, 0:GRAD_ROWS].astype(F32)
        parts = []
        for low in range(6):
            part = total[PIECE * low : PIECE * low + PIECE]
            start = 60 * (6 * x + low)
            if start < 480:
                halves = [edge_sum_ref[start + 30 * c : start + 30 * c + 32] for c in range(2)]
                part = part + pack(choose(*halves))
            parts.append(part)
        send_ref[x, 0:GRAD_ROWS] = jnp.concatenate(parts, axis=0).astype(BF16)
        send_ref[x, GRAD_ROWS:SEND_ONE] = rows_ref[...]


def first_sum_kernel(got_ref, send_ref):
    total = got_ref[0, 0:GRAD_ROWS].astype(F32)
    tail = got_ref[0, GRAD_ROWS + 16 : SEND_ONE].astype(F32)
    for x in range(1, 4):
        total = total + got_ref[x, 0:GRAD_ROWS].astype(F32)
        tail = tail + got_ref[x, GRAD_ROWS + 16 : SEND_ONE].astype(F32)
    total = total.astype(BF16)
    tail = tail.astype(BF16)
    heads = [got_ref[x, GRAD_ROWS : GRAD_ROWS + 16] for x in range(4)]
    for low in range(6):
        for high in range(2):
            n = 2 * low + high
            send_ref[n, 0:PIECE] = total[PIECE * low : PIECE * low + PIECE]
            for x in range(4):
                send_ref[n, PIECE + 16 * x : PIECE + 16 * x + 16] = heads[x]
            send_ref[n, PIECE + 64 : SEND_TWO] = tail


def second_sum_kernel(got_ref, send_ref):
    total = got_ref[0, 0:PIECE].astype(F32)
    for n in range(1, 12):
        total = total + got_ref[n, 0:PIECE].astype(F32)
    total = total.astype(BF16)
    for n in range(16):
        send_ref[n] = total


def conv_kernel(
    even_ref, odd_ref, taps_ref, below_ref, above_ref, own_ref, other_ref,
    out_ref, grad_ref,
    kernel_ref, shift_ref, roll_ref,
):
    core = lax.axis_index("core")
    for x in range(4):
        for low in range(6):
            for c in range(2):
                for high in range(2):
                    n = 2 * low + high
                    own = own_ref[n, PIECE:SEND_TWO].astype(F32)
                    other = other_ref[n, PIECE:SEND_TWO].astype(F32)
                    block = jnp.where(core == c, own, other)
                    start = 60 * (6 * x + low) + 15 * (2 * c + high)
                    kernel_ref[start : start + 16] = jnp.concatenate(
                        [block[16 * x : 16 * x + 16], block[64:80, 32 * x : 32 * x + 32]], axis=1
                    )

    def tap(r, s):
        row = (3 * r + s) * C
        return kernel_ref[row : row + C].astype(BF16)

    def dot(left, right):
        return jnp.dot(left, right, preferred_element_type=F32)

    def dot_t(left, right):
        return lax.dot_general(left, right, (((1,), (1,)), ((), ())), preferred_element_type=F32)

    zeros = jnp.zeros((8, C), BF16)
    even = even_ref[...]
    odd = odd_ref[...]
    odd_before = jnp.concatenate([zeros, odd[0:248]], axis=0)
    start_row = lax.broadcasted_iota(jnp.int32, (256, C), 0) % 8 == 0

    def down(columns, above):
        shift_ref[8:264] = columns.astype(F32)
        top = jnp.dot(every(0, True), above, preferred_element_type=F32)
        return jnp.where(start_row, top, shift_ref[7:263]).astype(BF16)

    shift_ref[0:8] = jnp.zeros((8, C), F32)
    even_down = down(even, above_ref[0])
    odd_down = down(odd, above_ref[1])
    odd_down_before = jnp.concatenate([zeros, odd_down[0:248]], axis=0)
    roll_ref[0:256] = dot(even, tap(2, 1)) + dot(odd, tap(2, 2)) + dot(odd_before, tap(2, 0))
    roll_ref[256:264] = jnp.zeros((8, C), F32)
    total = dot(even_down, tap(0, 1)) + dot(odd_down, tap(0, 2)) + dot(odd_down_before, tap(0, 0))
    total = total + dot(even, tap(1, 1)) + dot(odd, tap(1, 2)) + dot(odd_before, tap(1, 0))
    total = total + roll_ref[1:257]
    for g in range(8):
        wide = jnp.concatenate(
            [total[32 * g + 8 * k : 32 * g + 8 * k + 8] for k in range(4)], axis=1
        )
        rows = jnp.concatenate([wide[2 * i : 2 * i + 1] for i in range(4)], axis=0)
        out_ref[:, 640 * g : 640 * g + 640] = rows.astype(BF16)
    taps = [taps_ref[r] for r in range(3)]
    last = jnp.dot(every(7, True), below_ref[...], preferred_element_type=F32)
    taps[0] = (taps[0].astype(F32) + last).astype(BF16)
    after = [jnp.concatenate([t[8:256], zeros], axis=0) for t in taps]
    grad_even = dot_t(taps[0], tap(0, 1)) + dot_t(taps[1], tap(1, 1)) + dot_t(taps[2], tap(2, 1))
    grad_odd = dot_t(taps[0], tap(0, 2)) + dot_t(taps[1], tap(1, 2)) + dot_t(taps[2], tap(2, 2))
    for r in range(3):
        grad_odd = grad_odd + dot_t(after[r], tap(r, 0))
    for g in range(16):
        parts = []
        for k in range(2):
            row = 16 * g + 8 * k
            parts += [grad_even[row : row + 8], grad_odd[row : row + 8]]
        grad_ref[:, 640 * g : 640 * g + 640] = jnp.concatenate(parts, axis=1).astype(BF16)


def adam_kernel(got_ref, weight_ref, one_ref, two_ref, new_weight_ref, new_one_ref, new_two_ref, sums_ref):
    for core in range(2):
        total = got_ref[core].astype(F32)
        for y in range(1, 8):
            total = total + got_ref[2 * y + core].astype(F32)
        sums_ref[30 * core : 30 * core + 32] = unpack(total)
    gradient = sums_ref[0:60] / float(COUNT)
    weight = weight_ref[...]
    new_one = beta_one * one_ref[...] + (1.0 - beta_one) * gradient
    new_two = beta_two * two_ref[...] + (1.0 - beta_two) * gradient * gradient
    first_hat = new_one / (1.0 - beta_one**adam_step)
    second_hat = new_two / (1.0 - beta_two**adam_step)
    new_weight_ref[...] = weight - learn_rate * (
        first_hat / (jnp.sqrt(second_hat) + epsilon) + decay_rate * weight
    )
    new_one_ref[...] = new_one
    new_two_ref[...] = new_two


def body(image, cotangent, weight, moment_one, moment_two):
    shape = jax.ShapeDtypeStruct
    image = image.reshape(8, 64 * C)
    cotangent = cotangent.reshape(4, 32 * C)
    even, odd, strip, rows, edge, trade = call(
        prepare_kernel,
        [
            shape((256, C), BF16),
            shape((256, C), BF16),
            shape((4, 32 * C), BF16),
            shape((32, 128), BF16),
            shape((3, PIECE, 128), BF16),
            shape((2, PIECE, 128), BF16),
        ],
        [
            pltpu.VMEM((8, 64 * C), BF16),
            pltpu.VMEM((60, C), F32),
            pltpu.VMEM((64, C), F32),
            pltpu.SemaphoreType.DMA((3,)),
        ],
        [pl.BlockSpec(memory_space=pltpu.HBM)] * 3,
    )(*[pltpu.with_memory_space_constraint(a, pltpu.HBM) for a in (image, cotangent, weight)])
    route = [(i, i - 1 if i % 2 == 0 else i + 1) for i in range(1, 31)]
    traded = lax.ppermute(trade, ("zhi", "yhi", "ylo", "core"), route)
    keep, give, taps = call(
        grad_kernel,
        [
            shape((4, GRAD_ROWS, 128), BF16),
            shape((4, SWAP_ROWS, 128), BF16),
            shape((3, 256, C), BF16),
        ],
        [
            pltpu.VMEM((8, 32 * C), F32),
            pltpu.VMEM((24, 32 * C), F32),
            pltpu.VMEM((1448, C), F32),
        ],
    )(even, odd, strip, edge)
    given = lax.ppermute(give, "core", [(0, 1), (1, 0)])
    send_one, below, above = call(
        core_sum_kernel,
        [shape((4, SEND_ONE, 128), BF16), shape((32, C), BF16), shape((2, 32, C), BF16)],
        [pltpu.VMEM((512, C), F32)],
    )(keep, given, rows, edge, traded)
    got_one = lax.all_to_all(send_one, "x", 0, 0, tiled=True)
    send_two = call(first_sum_kernel, shape((12, SEND_TWO, 128), BF16))(got_one)
    got_two = lax.all_to_all(send_two, ("zlo", "zhi"), 0, 0, tiled=True)
    other = lax.ppermute(got_two, "core", [(0, 1), (1, 0)])
    send_three = call(second_sum_kernel, shape((16, PIECE, 128), BF16))(got_two)
    got_three = lax.all_to_all(send_three, ("ylo", "yhi", "core"), 0, 0, tiled=True)
    output, grad_image = call(
        conv_kernel,
        [shape((4, 32 * C), BF16), shape((8, 64 * C), BF16)],
        [
            pltpu.VMEM((1448, C), F32),
            pltpu.VMEM((264, C), F32),
            pltpu.VMEM((264, C), F32),
        ],
    )(even, odd, taps, below, above, got_two, other)
    new_weight, new_one, new_two = call(
        adam_kernel, [shape((60, C), F32)] * 3, [pltpu.VMEM((64, C), F32)]
    )(got_three, weight, moment_one, moment_two)
    return (output[None], grad_image[None], new_weight, new_one, new_two)


def solution(mesh):
    fine = Mesh(mesh.devices.reshape(4, 6, 2, 2, 4, 2), ("x", "zlo", "zhi", "yhi", "ylo", "core"))
    dp, space = ("x", "zlo"), ("zhi", "yhi", "ylo", "core")
    specs = (P(dp, space, None), P(dp, space, None), P(dp, None), P(dp, None), P(dp, None))

    return jax.shard_map(body, mesh=fine, in_specs=specs, out_specs=specs, check_vma=False)
```

```python
import jax
import jax.numpy as jnp
from jax import lax
from jax.experimental import pallas as pl
from jax.experimental.pallas import tpu as pltpu
from jax.sharding import Mesh
from jax.sharding import PartitionSpec as P


beta_one = 0.9
beta_two = 0.999
learn_rate = 0.01
decay_rate = 0.01
epsilon = 1e-08
adam_step = 10

C = 160
COUNT = 98304
F32 = jnp.float32
BF16 = jnp.bfloat16
VM = pl.BlockSpec(memory_space=pltpu.VMEM)

PIECE = 40
GRAD_ROWS = 6 * PIECE
SEND_ONE = GRAD_ROWS + 32
SEND_TWO = PIECE + 80
SWAP_ROWS = GRAD_ROWS + PIECE


def call(kernel, outs, scratch=(), ins=None, limit=16):
    one = not isinstance(outs, list)
    more = {} if ins is None else {"in_specs": ins}
    return pl.pallas_call(
        kernel,
        **more,
        out_shape=outs,
        out_specs=VM if one else [VM] * len(outs),
        scratch_shapes=list(scratch),
        compiler_params=pltpu.CompilerParams(vmem_limit_bytes=limit << 20),
    )


def tile_rows(piece, wide, groups):
    tiles = []
    for g in range(groups):
        block = piece(wide, g)
        tiles += [block[:, 160 * k : 160 * k + 160] for k in range(4)]
    return tiles


def read_block(ref, g):
    return ref[:, 640 * g : 640 * g + 640].astype(F32)


def every(offset, across=False):
    shape, short, long = ((256, 32), 1, 0) if across else ((32, 256), 0, 1)
    hit = lax.broadcasted_iota(jnp.int32, shape, long) == 8 * lax.broadcasted_iota(
        jnp.int32, shape, short
    ) + offset
    return hit.astype(F32).astype(BF16)


def pack(rows):
    tail = rows[:, 128:160]
    side = jnp.concatenate([tail[8 * b : 8 * b + 8] for b in range(4)], axis=1)
    return jnp.concatenate([rows[:, 0:128], side], axis=0)


def unpack(piece):
    side = piece[32:40]
    tail = jnp.concatenate([side[:, 32 * b : 32 * b + 32] for b in range(4)], axis=0)
    return jnp.concatenate([piece[0:32], tail], axis=1)


def prepare_kernel(
    image_hbm, cotan_hbm, weight_hbm,
    even_ref, odd_ref, cotan_ref, rows_ref, edge_ref, trade_ref,
    image_ref, own_ref, weight_ref, done,
):
    reads = [
        pltpu.make_async_copy(image_hbm, image_ref, done.at[0]),
        pltpu.make_async_copy(cotan_hbm, cotan_ref, done.at[1]),
        pltpu.make_async_copy(weight_hbm, own_ref, done.at[2]),
    ]
    for read in reads:
        read.start()
    for read in reads:
        read.wait()
    tiles = tile_rows(read_block, image_ref, 16)
    even = jnp.concatenate(tiles[0::2], axis=0).astype(BF16)
    odd = jnp.concatenate(tiles[1::2], axis=0).astype(BF16)
    even_ref[...] = even
    odd_ref[...] = odd
    flat = cotan_ref[...].astype(F32)
    edges = [
        jnp.dot(every(7), even, preferred_element_type=F32),
        jnp.dot(every(7), odd, preferred_element_type=F32),
        jnp.concatenate([flat[0:1, C * j : C * j + C] for j in range(32)], axis=0),
    ]
    for k in range(3):
        edge_ref[k] = pack(edges[k]).astype(BF16)
    first = lax.axis_index("core") == 0
    trade_ref[0] = jnp.where(first, edge_ref[2].astype(F32), edge_ref[0].astype(F32)).astype(BF16)
    trade_ref[1] = edge_ref[1]
    weight_ref[0:60] = own_ref[...]
    weight_ref[60:64] = jnp.zeros((4, C), F32)
    quarter = 2 * lax.axis_index("core") + lax.axis_index("zhi")
    mine = weight_ref[0:16]
    for q in range(1, 4):
        mine = jnp.where(quarter == q, weight_ref[15 * q : 15 * q + 16], mine)
    tail = mine[:, 128:160]
    lane = lax.broadcasted_iota(jnp.int32, (16, 128), 1) // 32
    tail = jnp.where(lane == 2 * lax.axis_index("xhi") + lax.axis_index("xlo"), jnp.concatenate([tail] * 4, axis=1), 0.0)
    rows_ref[...] = jnp.concatenate([mine[:, 0:128], tail], axis=0).astype(BF16)


def grad_kernel(
    even_ref, odd_ref, cotan_ref, edge_ref,
    keep_ref, give_ref, taps_ref,
    five_ref, spread_ref, sums_ref,
):
    even = even_ref[...]
    odd = odd_ref[...]
    five_ref[...] = jnp.zeros_like(five_ref)
    five_ref[0:4] = cotan_ref[...].astype(F32)
    out_row = lax.broadcasted_iota(jnp.int32, (24, 8), 0)
    in_row = lax.broadcasted_iota(jnp.int32, (24, 8), 1)
    pick = (2 * in_row + out_row // 8 - 1 == out_row % 8).astype(F32).astype(BF16)
    spread_ref[...] = jnp.dot(pick, five_ref[...].astype(BF16), preferred_element_type=F32)
    taps = []
    for r in range(3):
        cols = tile_rows(lambda ref, g: ref[8 * r : 8 * r + 8, 640 * g : 640 * g + 640], spread_ref, 8)
        block = jnp.concatenate(cols, axis=0).astype(BF16)
        taps_ref[r] = block
        taps.append(block)
    zeros = jnp.zeros((8, C), BF16)

    def put(r, s, left, right):
        row = (3 * r + s) * C
        sums_ref[row : row + C] = lax.dot_general(
            left, right, (((0,), (0,)), ((), ())), preferred_element_type=F32
        )

    for r in range(3):
        put(r, 1, even, taps[r])
        put(r, 2, odd, taps[r])
        put(r, 0, odd[0:248], taps[r][8:256])
    sums_ref[1440:1448] = zeros.astype(F32)
    first = lax.axis_index("core") == 0
    for x in range(4):
        for low in range(6):
            start = 60 * (6 * x + low)
            halves = [pack(sums_ref[start + 30 * c : start + 30 * c + 32]) for c in range(2)]
            at = slice(PIECE * low, PIECE * low + PIECE)
            keep_ref[x, at] = jnp.where(first, halves[0], halves[1]).astype(BF16)
            give_ref[x, at] = jnp.where(first, halves[1], halves[0]).astype(BF16)
    for k in range(3):
        give_ref[k, GRAD_ROWS:SWAP_ROWS] = edge_ref[k]
    give_ref[3, GRAD_ROWS:SWAP_ROWS] = edge_ref[2]


def core_sum_kernel(
    keep_ref, got_ref, rows_ref, edge_ref, trade_ref,
    send_ref, below_ref, above_ref,
    edge_sum_ref,
):
    first = lax.axis_index("core") == 0
    mine = [unpack(edge_ref[k].astype(F32)) for k in range(3)]
    partner = [unpack(got_ref[k, GRAD_ROWS:SWAP_ROWS].astype(F32)) for k in range(3)]
    far = [unpack(trade_ref[k].astype(F32)) for k in range(2)]

    def choose(zero, one):
        return jnp.where(first, zero, one)

    inner_cotan, outer_cotan = choose(partner[2], mine[2]), choose(mine[2], far[0])
    zero = jnp.zeros((1, C), F32)
    rights = [
        jnp.concatenate([inner_cotan[1:32], zero, outer_cotan[1:32], zero], axis=0).astype(BF16),
        jnp.concatenate([inner_cotan, outer_cotan], axis=0).astype(BF16),
    ]
    even, odd = [
        jnp.concatenate(
            [choose(mine[k], partner[k]), choose(far[k], mine[k])], axis=0
        ).astype(BF16)
        for k in range(2)
    ]
    below_ref[...] = choose(partner[2], far[0]).astype(BF16)
    for k in range(2):
        above_ref[k] = choose(far[k], partner[k]).astype(BF16)
    edge_sum_ref[480:512] = jnp.zeros((32, C), F32)
    for s, left in ((0, odd), (1, even), (2, odd)):
        edge_sum_ref[C * s : C * s + C] = lax.dot_general(
            left, rights[min(s, 1)], (((0,), (0,)), ((), ())), preferred_element_type=F32
        )
    for x in range(4):
        total = keep_ref[x].astype(F32) + got_ref[x, 0:GRAD_ROWS].astype(F32)
        parts = []
        for low in range(6):
            part = total[PIECE * low : PIECE * low + PIECE]
            start = 60 * (6 * x + low)
            if start < 480:
                halves = [edge_sum_ref[start + 30 * c : start + 30 * c + 32] for c in range(2)]
                part = part + pack(choose(*halves))
            parts.append(part)
        send_ref[2 * (x % 2) + x // 2, 0:GRAD_ROWS] = jnp.concatenate(parts, axis=0).astype(BF16)
        send_ref[2 * (x % 2) + x // 2, GRAD_ROWS:SEND_ONE] = rows_ref[...]


def first_sum_kernel(got_ref, send_ref):
    total = got_ref[0, 0:GRAD_ROWS].astype(F32)
    tail = got_ref[0, GRAD_ROWS + 16 : SEND_ONE].astype(F32)
    for x in range(1, 4):
        total = total + got_ref[x, 0:GRAD_ROWS].astype(F32)
        tail = tail + got_ref[x, GRAD_ROWS + 16 : SEND_ONE].astype(F32)
    total = total.astype(BF16)
    tail = tail.astype(BF16)
    heads = [got_ref[2 * (x % 2) + x // 2, GRAD_ROWS : GRAD_ROWS + 16] for x in range(4)]
    for low in range(6):
        for high in range(2):
            n = 2 * low + high
            send_ref[n, 0:PIECE] = total[PIECE * low : PIECE * low + PIECE]
            for x in range(4):
                send_ref[n, PIECE + 16 * x : PIECE + 16 * x + 16] = heads[x]
            send_ref[n, PIECE + 64 : SEND_TWO] = tail


def second_sum_kernel(got_ref, send_ref):
    total = got_ref[0, 0:PIECE].astype(F32)
    for n in range(1, 12):
        total = total + got_ref[n, 0:PIECE].astype(F32)
    total = total.astype(BF16)
    for n in range(16):
        send_ref[n] = total


def conv_kernel(
    even_ref, odd_ref, taps_ref, below_ref, above_ref, own_ref, other_ref,
    out_ref, grad_ref,
    kernel_ref, shift_ref, roll_ref,
):
    core = lax.axis_index("core")
    for x in range(4):
        for low in range(6):
            for c in range(2):
                for high in range(2):
                    n = 2 * low + high
                    own = own_ref[n, PIECE:SEND_TWO].astype(F32)
                    other = other_ref[n, PIECE:SEND_TWO].astype(F32)
                    block = jnp.where(core == c, own, other)
                    start = 60 * (6 * x + low) + 15 * (2 * c + high)
                    kernel_ref[start : start + 16] = jnp.concatenate(
                        [block[16 * x : 16 * x + 16], block[64:80, 32 * x : 32 * x + 32]], axis=1
                    )

    def tap(r, s):
        row = (3 * r + s) * C
        return kernel_ref[row : row + C].astype(BF16)

    def dot(left, right):
        return jnp.dot(left, right, preferred_element_type=F32)

    def dot_t(left, right):
        return lax.dot_general(left, right, (((1,), (1,)), ((), ())), preferred_element_type=F32)

    zeros = jnp.zeros((8, C), BF16)
    even = even_ref[...]
    odd = odd_ref[...]
    odd_before = jnp.concatenate([zeros, odd[0:248]], axis=0)
    start_row = lax.broadcasted_iota(jnp.int32, (256, C), 0) % 8 == 0

    def down(columns, above):
        shift_ref[8:264] = columns.astype(F32)
        top = jnp.dot(every(0, True), above, preferred_element_type=F32)
        return jnp.where(start_row, top, shift_ref[7:263]).astype(BF16)

    shift_ref[0:8] = jnp.zeros((8, C), F32)
    even_down = down(even, above_ref[0])
    odd_down = down(odd, above_ref[1])
    odd_down_before = jnp.concatenate([zeros, odd_down[0:248]], axis=0)
    roll_ref[0:256] = dot(even, tap(2, 1)) + dot(odd, tap(2, 2)) + dot(odd_before, tap(2, 0))
    roll_ref[256:264] = jnp.zeros((8, C), F32)
    total = dot(even_down, tap(0, 1)) + dot(odd_down, tap(0, 2)) + dot(odd_down_before, tap(0, 0))
    total = total + dot(even, tap(1, 1)) + dot(odd, tap(1, 2)) + dot(odd_before, tap(1, 0))
    total = total + roll_ref[1:257]
    for g in range(8):
        wide = jnp.concatenate(
            [total[32 * g + 8 * k : 32 * g + 8 * k + 8] for k in range(4)], axis=1
        )
        rows = jnp.concatenate([wide[2 * i : 2 * i + 1] for i in range(4)], axis=0)
        out_ref[:, 640 * g : 640 * g + 640] = rows.astype(BF16)
    taps = [taps_ref[r] for r in range(3)]
    last = jnp.dot(every(7, True), below_ref[...], preferred_element_type=F32)
    taps[0] = (taps[0].astype(F32) + last).astype(BF16)
    after = [jnp.concatenate([t[8:256], zeros], axis=0) for t in taps]
    grad_even = dot_t(taps[0], tap(0, 1)) + dot_t(taps[1], tap(1, 1)) + dot_t(taps[2], tap(2, 1))
    grad_odd = dot_t(taps[0], tap(0, 2)) + dot_t(taps[1], tap(1, 2)) + dot_t(taps[2], tap(2, 2))
    for r in range(3):
        grad_odd = grad_odd + dot_t(after[r], tap(r, 0))
    for g in range(16):
        parts = []
        for k in range(2):
            row = 16 * g + 8 * k
            parts += [grad_even[row : row + 8], grad_odd[row : row + 8]]
        grad_ref[:, 640 * g : 640 * g + 640] = jnp.concatenate(parts, axis=1).astype(BF16)


def adam_kernel(got_ref, weight_ref, one_ref, two_ref, new_weight_ref, new_one_ref, new_two_ref, sums_ref):
    for core in range(2):
        total = got_ref[core].astype(F32)
        for y in range(1, 8):
            total = total + got_ref[2 * y + core].astype(F32)
        sums_ref[30 * core : 30 * core + 32] = unpack(total)
    gradient = sums_ref[0:60] / float(COUNT)
    weight = weight_ref[...]
    new_one = beta_one * one_ref[...] + (1.0 - beta_one) * gradient
    new_two = beta_two * two_ref[...] + (1.0 - beta_two) * gradient * gradient
    first_hat = new_one / (1.0 - beta_one**adam_step)
    second_hat = new_two / (1.0 - beta_two**adam_step)
    new_weight_ref[...] = weight - learn_rate * (
        first_hat / (jnp.sqrt(second_hat) + epsilon) + decay_rate * weight
    )
    new_one_ref[...] = new_one
    new_two_ref[...] = new_two


def body(image, cotangent, weight, moment_one, moment_two):
    shape = jax.ShapeDtypeStruct
    image = image.reshape(8, 64 * C)
    cotangent = cotangent.reshape(4, 32 * C)
    even, odd, strip, rows, edge, trade = call(
        prepare_kernel,
        [
            shape((256, C), BF16),
            shape((256, C), BF16),
            shape((4, 32 * C), BF16),
            shape((32, 128), BF16),
            shape((3, PIECE, 128), BF16),
            shape((2, PIECE, 128), BF16),
        ],
        [
            pltpu.VMEM((8, 64 * C), BF16),
            pltpu.VMEM((60, C), F32),
            pltpu.VMEM((64, C), F32),
            pltpu.SemaphoreType.DMA((3,)),
        ],
        [pl.BlockSpec(memory_space=pltpu.HBM)] * 3,
    )(*[pltpu.with_memory_space_constraint(a, pltpu.HBM) for a in (image, cotangent, weight)])
    route = [(i, i - 1 if i % 2 == 0 else i + 1) for i in range(1, 31)]
    traded = lax.ppermute(trade, ("zhi", "y", "core"), route)
    keep, give, taps = call(
        grad_kernel,
        [
            shape((4, GRAD_ROWS, 128), BF16),
            shape((4, SWAP_ROWS, 128), BF16),
            shape((3, 256, C), BF16),
        ],
        [
            pltpu.VMEM((8, 32 * C), F32),
            pltpu.VMEM((24, 32 * C), F32),
            pltpu.VMEM((1448, C), F32),
        ],
    )(even, odd, strip, edge)
    given = lax.ppermute(give, "core", [(0, 1), (1, 0)])
    send_one, below, above = call(
        core_sum_kernel,
        [shape((4, SEND_ONE, 128), BF16), shape((32, C), BF16), shape((2, 32, C), BF16)],
        [pltpu.VMEM((512, C), F32)],
    )(keep, given, rows, edge, traded)
    got_one = lax.all_to_all(send_one, ("xlo", "xhi"), 0, 0, tiled=True)
    send_two = call(first_sum_kernel, shape((12, SEND_TWO, 128), BF16))(got_one)
    got_two = lax.all_to_all(send_two, ("zlo", "zhi"), 0, 0, tiled=True)
    other = lax.ppermute(got_two, "core", [(0, 1), (1, 0)])
    send_three = call(second_sum_kernel, shape((16, PIECE, 128), BF16))(got_two)
    got_three = lax.all_to_all(send_three, ("y", "core"), 0, 0, tiled=True)
    output, grad_image = call(
        conv_kernel,
        [shape((4, 32 * C), BF16), shape((8, 64 * C), BF16)],
        [
            pltpu.VMEM((1448, C), F32),
            pltpu.VMEM((264, C), F32),
            pltpu.VMEM((264, C), F32),
        ],
    )(even, odd, taps, below, above, got_two, other)
    new_weight, new_one, new_two = call(
        adam_kernel, [shape((60, C), F32)] * 3, [pltpu.VMEM((64, C), F32)]
    )(got_three, weight, moment_one, moment_two)
    return (output[None], grad_image[None], new_weight, new_one, new_two)


def solution(mesh):
    fine = Mesh(mesh.devices.reshape(2, 2, 6, 2, 8, 2), ("xhi", "xlo", "zlo", "zhi", "y", "core"))
    dp, space = ("xhi", "xlo", "zlo"), ("zhi", "y", "core")
    specs = (P(dp, space, None), P(dp, space, None), P(dp, None), P(dp, None), P(dp, None))

    return jax.shard_map(body, mesh=fine, in_specs=specs, out_specs=specs, check_vma=False)
```
